512 devices in a mesh: tr: 64 (over x, z), ct: 8 (over y, core).
Axes of the slice: x: 4, y: 4, z: 16, core: 2. Of those that a mesh axis runs over, the one named last changes fastest.
Arguments:
- amplitudes: bfloat16 [8, 4096, 2, 4096], P(None, 'tr', None, 'ct'), may hold values from -6 to 6
- cycle_integrals: bfloat16 [2, 4096, 1, 4096], P(None, 'ct', None, 'tr'), may hold values from -0.0625 to 0.0625
- pair_live: int32 [8, 64], replicated, may hold values 0 or 1
Outputs:
- permuted: bfloat16 [8, 4096, 1, 4096], P('ct', 'tr')
The draws below stay inside these ranges and needn't reach their ends.
All inputs are finite; a program needn't handle non-finite values.
Results may differ from the reference program's by a relative error of at most 0.017.
Values may be sent and summed in bfloat16 or wider, within the bound.
A program may use at most 64 MiB of HBM per device.

```python
import jax
import jax.numpy as jnp
from jax import lax

VT = 64
NI = 8
NK = 2
NJ = 1
NV = 64
V = 4096
N_CT = 8


def set_ends(result, own_key, smallest, top_value):
    spot = [jax.random.randint(jax.random.fold_in(own_key, axis), (), 0, length) for axis, length in enumerate(result.shape)]
    longest = result.shape.index(max(result.shape))
    neighbour = spot[:longest] + [(spot[longest] + 1) % result.shape[longest]] + spot[longest + 1:]
    return result.at[tuple(spot)].set(smallest).at[tuple(neighbour)].set(top_value)


def with_spikes(result, own_key, source, target, parts, factor):
    owner, partner = [(jnp.arange(result.shape[axis_at]) // (result.shape[axis_at] // parts)).reshape([-1 if axis == axis_at else 1 for axis in range(result.ndim)]) for axis_at in (source, target)]
    chosen = jax.random.permutation(own_key, parts)[partner]
    strong = (owner == chosen) | (owner == (partner + parts // 2) % parts)
    return jnp.where(strong, factor * result, result)


def level_of(key, extent, pieces, smallest, high):
    loudness, own = 1.0, jax.random.fold_in(key, 6)
    for dim, blocks in pieces:
        heights = jnp.exp(jax.random.uniform(jax.random.fold_in(own, dim), (blocks,), jnp.float32, smallest / len(pieces), high / len(pieces)))
        loudness = loudness * jnp.repeat(heights, extent[dim] // blocks).reshape([-1 if axis == dim else 1 for axis in range(len(extent))])
    return loudness


def bell_draw(rng, shape, width, bound, cuts=(), kind=jnp.bfloat16):
    gain = level_of(rng, shape, cuts, -0.22, 0.18) if cuts else 1.0
    result = jax.random.normal(rng, shape, jnp.float32) * width * gain
    return jnp.minimum(jnp.maximum(result, -bound), bound).astype(kind)


def heavy_noise(own_key, dims, deviation, bound, cuts, heavy, dtype=jnp.bfloat16):
    result = deviation * jax.random.normal(own_key, dims, jnp.float32)
    if cuts:
        result = result * level_of(own_key, dims, cuts, -0.22, 0.18)
    return jnp.clip(with_spikes(result, jax.random.fold_in(own_key, 3), *heavy), -bound, bound).astype(dtype)


def setup_inputs(seed: int = 0) -> dict:
    keys = jax.random.split(jax.random.key(seed), 4)
    amplitudes = heavy_noise(keys[0], (NI, V, NK, V), 1.0, 6.0, ((1, 64), (3, 8)), (3, 0, 8, 2.0))
    cycle_integrals = bell_draw(keys[1], (NK, V, NJ, V), (NK * V) ** -0.5, 0.0625, ((1, 8), (3, 64)))
    pair_live = set_ends((jax.random.randint(keys[2], (NI, NV), 0, 4) < 3).astype(jnp.int32), jax.random.fold_in(keys[2], 1), 0, 1)
    return {"amplitudes": amplitudes, "cycle_integrals": cycle_integrals, "pair_live": pair_live}


def reference(amplitudes, cycle_integrals, pair_live):
    row_live = jnp.repeat(pair_live, VT, axis=1).astype(jnp.bfloat16)
    col_live = row_live[:NK]
    masked = amplitudes * row_live[:, :, None, None] * col_live[None, None, :, :]
    per_block = V // N_CT

    def block_term(group, totals):
        offset = (group * per_block).astype(jnp.int32)
        amp_blk = lax.dynamic_slice_in_dim(masked, offset, per_block, 3).astype(jnp.float32)
        int_blk = lax.dynamic_slice_in_dim(cycle_integrals, offset, per_block, 1).astype(jnp.float32)
        product = jnp.einsum('iakc,kcjb->iajb', amp_blk, int_blk)
        rounded = lax.optimization_barrier(product.astype(jnp.bfloat16))
        return totals + rounded.astype(jnp.float32)

    start_sum = jnp.zeros((NI, V, NJ, V), jnp.float32)
    totals = lax.fori_loop(jnp.int32(0), jnp.int32(N_CT), block_term, start_sum)
    cycle = totals.astype(jnp.bfloat16)
    return jnp.transpose(cycle, (0, 3, 2, 1))
```

```python
import functools

import jax
import jax.numpy as jnp
from jax import lax
from jax.experimental import pallas as pl
from jax.experimental.pallas import tpu as pltpu
from jax.sharding import PartitionSpec as P

MESH = pl.DeviceIdType.MESH
F32 = jnp.float32
BF16 = jnp.bfloat16
NZ = 16


def dot_nt(lhs, rhs):
    return lax.dot_general(lhs, rhs, (((1,), (1,)), ((), ())), preferred_element_type=F32)


def kernel(
    a_ref, w_ref, out_ref,
    abuf, wbuf, kept, csend, crecv, y1send, y1recv, y2send, y2recv, psend, pieces,
    s_a, s_af, r_a, s_w, r_w, s_c, r_c, s_y1, r_y1, s_y2, r_y2, s_p, r_p,
):
    t_index = lax.axis_index("tr")
    c_index = lax.axis_index("ct")
    x, z = t_index // NZ, t_index % NZ
    y, q = c_index // 2, c_index % 2
    yn1 = y + 1 - 2 * (y % 2)
    yn3 = 3 - y
    yop = (y + 2) % 4

    def dev(xx, yy, zz, qq):
        return (xx * NZ + zz, yy * 2 + qq)

    xp, xm = dev((x + 1) % 4, y, z, q), dev((x + 3) % 4, y, z, q)
    zp, zm = dev(x, y, (z + 1) % NZ, q), dev(x, y, (z + NZ - 1) % NZ, q)
    mate = dev(x, y, z, 1 - q)

    def rcopy(src, dst, ssem, rsem, to):
        return pltpu.make_async_remote_copy(
            src_ref=src, dst_ref=dst, send_sem=ssem, recv_sem=rsem, device_id=to, device_id_type=MESH
        )

    barrier = pltpu.get_barrier_semaphore()

    def greet(n, carry):
        zz, qq = n // 2, n % 2

        @pl.when(n != z * 2 + q)
        def _():
            pl.semaphore_signal(barrier, inc=1, device_id=dev(x, y, zz, qq), device_id_type=MESH)

        return carry

    for other in (xp, xm, dev(x, yn1, z, q), dev(x, yn3, z, q)):
        pl.semaphore_signal(barrier, inc=1, device_id=other, device_id_type=MESH)
    lax.fori_loop(0, 2 * NZ, greet, 0)
    pl.semaphore_wait(barrier, 2 * NZ - 1 + 4)

    def a_own(side, chunk):
        rows = pl.ds(chunk * 128, 128)
        return rcopy(a_ref.at[:, rows], abuf.at[side, :, rows], s_a.at[side, chunk], r_a.at[side, chunk],
                     (xp, xm)[side])

    def a_fwd(side, chunk):
        rows = pl.ds(chunk * 128, 128)
        return rcopy(abuf.at[side, :, rows], abuf.at[2, :, rows], s_af.at[chunk], r_a.at[2, chunk],
                     (xp, xm)[side])

    def w_hop(way, step, half):
        src = w_ref.at[half] if step == 1 else wbuf.at[way, step - 2, half]
        dst = wbuf.at[1, 7, half] if step == 8 else wbuf.at[way, step - 1, half]
        return rcopy(src, dst, s_w.at[way, step - 1, half], r_w.at[way, step - 1, half], (zm, zp)[way])

    for half in range(2):
        for way in range(2):
            w_hop(way, 1, half).start()
    for order in range(4):
        a_own(0, order).start()
        a_own(1, (order + 2) % 4).start()
    wbuf[0, 7] = w_ref[...]

    def compute(t, h, blocks):
        def pair(p, carry):
            total = jnp.zeros((512, 256), F32)
            for k in range(2):
                mine = wbuf[q, pl.ds(h * 4, 4), k].reshape(256, 512)
                theirs = wbuf[1 - q, pl.ds(h * 4, 4), k].reshape(256, 512)
                rows = jnp.concatenate([mine, theirs], axis=0)
                total = total + dot_nt(rows, blocks[k, pl.ds(pl.multiple_of(p * 256, 256), 256)])
            for n in range(2):
                cols = total[:, n * 128:(n + 1) * 128]
                kept[t, p * 2 + n] = cols[:256]
                csend[t, p * 2 + n] = cols[256:].astype(BF16)
            return carry

        lax.fori_loop(0, 2, pair, 0)
        c_copy(t).start()

    def c_copy(t):
        return rcopy(csend.at[t], crecv.at[t], s_c.at[t], r_c.at[t], mate)

    def partners(h):
        return (1 - h) * yn1 + h * yn3, (1 - h) * yn3 + h * yn1

    def y1_copy(t, h):
        return rcopy(y1send.at[t], y1recv.at[t], s_y1.at[t], r_y1.at[t], dev(x, partners(h)[0], z, q))

    def y2_copy(t, h):
        return rcopy(y2send.at[t], y2recv.at[t], s_y2.at[t], r_y2.at[t], dev(x, partners(h)[1], z, q))

    def core_sum(t, h):
        c_copy(t).wait_recv()
        near, far = partners(h)
        y1send[t, 0] = (kept[t, near] + crecv[t, near].astype(F32)).astype(BF16)
        y1send[t, 1] = (kept[t, yop] + crecv[t, yop].astype(F32)).astype(BF16)
        y1_copy(t, h).start()
        kept[t, y] = kept[t, y] + crecv[t, y].astype(F32)
        kept[t, far] = kept[t, far] + crecv[t, far].astype(F32)

    def y_sum1(t, h):
        y1_copy(t, h).wait_recv()
        far = partners(h)[1]
        y2send[t] = (kept[t, far] + y1recv[t, 1].astype(F32)).astype(BF16)
        y2_copy(t, h).start()
        kept[t, y] = kept[t, y] + y1recv[t, 0].astype(F32)

    def target(h, s):
        slot = h * 4 + s
        off = (1 - q) * ((slot + 1) % 8) + q * (15 - slot)
        return (z + off) % NZ, slot

    def p_copy(t, h, stage, s, i):
        there = target(h, s)[0]
        return rcopy(psend.at[t, s, i], pieces.at[stage, z], s_p.at[t, s, i], r_p.at[stage, z],
                     dev(x, y, there, i))

    low = lax.broadcasted_iota(jnp.int32, (32, 128), 1) < 64

    def y_sum2(t, h, stage):
        y2_copy(t, h).wait_recv()
        for s in range(4):
            full = kept[t, y, s * 64:(s + 1) * 64] + y2recv[t, s * 64:(s + 1) * 64].astype(F32)
            top, bottom = full[:32], full[32:]
            psend[t, s, 0] = jnp.where(low, top, pltpu.roll(bottom, 64, 1)).astype(BF16)
            psend[t, s, 1] = jnp.where(low, pltpu.roll(top, 64, 1), bottom).astype(BF16)
        for s in range(4):
            own = (target(h, s)[1] == 7) & (q == 0)

            @pl.when(own)
            def _():
                pieces[stage, z] = psend[t, s, 0]

            @pl.when(jnp.logical_not(own))
            def _():
                p_copy(t, h, stage, s, 0).start()

            p_copy(t, h, stage, s, 1).start()

    def ring(step):
        for half in range(2):
            for way in range(2):
                w_hop(way, step - 1, half).wait_recv()
                if step < 8 or half == 1 - way:
                    w_hop(way, step, half).start()

    ring(2)
    ring(3)
    a_own(0, 0).wait_recv()
    a_fwd(0, 0).start()
    a_own(1, 2).wait_recv()
    a_fwd(1, 2).start()
    ring(4)
    ring(5)
    compute(0, 0, a_ref)
    a_own(0, 1).wait_recv()
    a_fwd(0, 1).start()
    a_own(1, 3).wait_recv()
    a_fwd(1, 3).start()
    ring(6)
    core_sum(0, 0)
    ring(7)
    y_sum1(0, 0)
    ring(8)
    y_sum2(0, 0, 0)
    w_hop(0, 8, 1).wait_recv()
    w_hop(1, 8, 0).wait_recv()
    compute(1, 1, a_ref)
    for chunk in range(2):
        a_own(0, chunk + 2).wait_recv()
        a_own(1, chunk).wait_recv()

    def step(t, carry):
        h, hh = t % 2, (t + 1) % 2

        @pl.when(t == 6)
        def _():
            for chunk in range(4):
                a_fwd(chunk // 2, chunk).wait_recv()

        @pl.when(t < 8)
        def _():
            compute(t, h, abuf.at[t // 2 - 1])

        @pl.when(t < 9)
        def _():
            core_sum(t - 1, hh)

        @pl.when((t > 2) & (t < 10))
        def _():
            y_sum1(t - 2, h)

        @pl.when(t > 3)
        def _():
            y_sum2(t - 3, hh, (t - 3) // 2)

        return carry

    lax.fori_loop(2, 11, step, 0)

    for stage in range(4):
        xs = (x + (0, 3, 1, 2)[stage]) % 4

        def arrive(n, carry):
            @pl.when((n != z) | (q != 0))
            def _():
                rcopy(psend.at[0, 0, 0], pieces.at[stage, n], s_p.at[0, 0, 0], r_p.at[stage, n],
                      mate).wait_recv()

            return carry

        lax.fori_loop(0, NZ, arrive, 0)
        for m in range(NZ // 2):
            even, odd = pieces[stage, 2 * m].astype(F32), pieces[stage, 2 * m + 1].astype(F32)
            cols = pl.ds(pl.multiple_of(xs * 1024 + m * 128, 128), 128)
            out_ref[0:32, cols] = jnp.where(low, even, pltpu.roll(odd, 64, 1)).astype(BF16)
            out_ref[32:64, cols] = jnp.where(low, pltpu.roll(even, 64, 1), odd).astype(BF16)

    for way in range(2):
        for n in range(1, 9):
            for half in range(2):
                if n < 8 or half == 1 - way:
                    w_hop(way, n, half).wait_send()
        for chunk in range(4):
            a_own(way, chunk).wait_send()
    for chunk in range(4):
        a_fwd(chunk // 2, chunk).wait_send()

    def drain(t, carry):
        h = t % 2
        c_copy(t).wait_send()
        y1_copy(t, h).wait_send()
        y2_copy(t, h).wait_send()
        for s in range(4):
            own = (target(h, s)[1] == 7) & (q == 0)

            @pl.when(jnp.logical_not(own))
            def _():
                p_copy(t, h, t // 2, s, 0).wait_send()

            p_copy(t, h, t // 2, s, 1).wait_send()
        return carry

    lax.fori_loop(0, 8, drain, 0)


def fused(blocks, tiles):
    dma = pltpu.SemaphoreType.DMA
    return pl.pallas_call(
        kernel,
        out_shape=jax.ShapeDtypeStruct((64, 4096), BF16),
        in_specs=[pl.BlockSpec(memory_space=pltpu.VMEM)] * 2,
        out_specs=pl.BlockSpec(memory_space=pltpu.VMEM),
        scratch_shapes=[
            pltpu.VMEM((3, 2, 512, 512), BF16),
            pltpu.VMEM((2, 8, 2, 64, 512), BF16),
            pltpu.VMEM((8, 4, 256, 128), F32),
            pltpu.VMEM((8, 4, 256, 128), BF16),
            pltpu.VMEM((8, 4, 256, 128), BF16),
            pltpu.VMEM((8, 2, 256, 128), BF16),
            pltpu.VMEM((8, 2, 256, 128), BF16),
            pltpu.VMEM((8, 256, 128), BF16),
            pltpu.VMEM((8, 256, 128), BF16),
            pltpu.VMEM((8, 4, 2, 32, 128), BF16),
            pltpu.VMEM((4, NZ, 32, 128), BF16),
            dma((2, 4)), dma((4,)), dma((3, 4)),
            dma((2, 8, 2)), dma((2, 8, 2)),
            dma((8,)), dma((8,)), dma((8,)), dma((8,)), dma((8,)), dma((8,)),
            dma((8, 4, 2)), dma((4, NZ)),
        ],
        compiler_params=pltpu.CompilerParams(
            collective_id=0, has_side_effects=True, vmem_limit_bytes=48 * 1024 * 1024
        ),
        name="cycle_fused",
    )(blocks, tiles)


def per_device(amplitudes, cycle_integrals, pair_live):
    row_index = lax.axis_index("tr")
    col_index = lax.axis_index("ct")
    row_live = lax.dynamic_slice_in_dim(pair_live, row_index, 1, 1).astype(BF16)
    col_full = jnp.repeat(pair_live[:2], 64, axis=1)
    col_live = lax.dynamic_slice_in_dim(col_full, col_index * 512, 512, 1).astype(BF16)
    masked = amplitudes * row_live[:, :, None, None] * col_live[None, None, :, :]
    blocks = masked.transpose(2, 0, 1, 3).reshape(2, 512, 512)
    tiles = cycle_integrals[:, :, 0, :].transpose(0, 2, 1)
    return fused(blocks, tiles).reshape(1, 64, 1, 4096)


def solution(mesh):
    return jax.shard_map(
        per_device,
        mesh=mesh,
        in_specs=(P(None, "tr", None, "ct"), P(None, "ct", None, "tr"), P()),
        out_specs=P("ct", "tr", None, None),
        check_vma=False,
    )
```

```python
import functools

import jax
import jax.numpy as jnp
from jax import lax
from jax.experimental import pallas as pl
from jax.experimental.pallas import tpu as pltpu
from jax.sharding import PartitionSpec as P

MESH = pl.DeviceIdType.MESH
F32 = jnp.float32
BF16 = jnp.bfloat16
NZ = 16


def dot_nt(lhs, rhs):
    return lax.dot_general(lhs, rhs, (((1,), (1,)), ((), ())), preferred_element_type=F32)


def kernel(
    a_hbm, w_hbm, live_hbm, out_ref,
    raw, live, aown, abuf, wbuf, kept, csend, crecv, y1send, y1recv, y2send, y2recv, psend, pieces,
    s_in, s_a, s_af, r_a, s_w, r_w, s_c, r_c, s_y1, r_y1, s_y2, r_y2, s_p, r_p,
):
    t_index = lax.axis_index("tr")
    c_index = lax.axis_index("ct")
    x, z = t_index // NZ, t_index % NZ
    y, q = c_index // 2, c_index % 2
    yn1 = y + 1 - 2 * (y % 2)
    yn3 = 3 - y
    yop = (y + 2) % 4

    def dev(xx, yy, zz, qq):
        return (xx * NZ + zz, yy * 2 + qq)

    xp, xm = dev((x + 1) % 4, y, z, q), dev((x + 3) % 4, y, z, q)
    zp, zm = dev(x, y, (z + 1) % NZ, q), dev(x, y, (z + NZ - 1) % NZ, q)
    mate = dev(x, y, z, 1 - q)
    ynear, yfar = dev(x, yn1, z, q), dev(x, yn3, z, q)

    def rcopy(src, dst, ssem, rsem, to):
        return pltpu.make_async_remote_copy(
            src_ref=src, dst_ref=dst, send_sem=ssem, recv_sem=rsem, device_id=to, device_id_type=MESH
        )

    barrier = pltpu.get_barrier_semaphore()
    for other in (zp, zm, xp, xm, mate, ynear, yfar):
        pl.semaphore_signal(barrier, inc=1, device_id=other, device_id_type=MESH)

    live_in = pltpu.make_async_copy(live_hbm, live, s_in.at[0])
    w_in = pltpu.make_async_copy(w_hbm, wbuf.at[0, 7], s_in.at[1])
    a_in = [
        pltpu.make_async_copy(a_hbm.at[pl.ds(2 * n, 2)], raw.at[pl.ds(2 * n, 2)], s_in.at[2 + n])
        for n in range(4)
    ]
    live_in.start()
    for n in (0, 2, 1, 3):
        a_in[n].start()
    w_in.start()

    def a_own(side, chunk):
        rows = pl.ds(chunk * 128, 128)
        return rcopy(aown.at[:, rows], abuf.at[side, :, rows], s_a.at[side, chunk], r_a.at[side, chunk],
                     (xp, xm)[side])

    def a_fwd(side, chunk):
        rows = pl.ds(chunk * 128, 128)
        return rcopy(abuf.at[side, :, rows], abuf.at[2, :, rows], s_af.at[chunk], r_a.at[2, chunk],
                     (xp, xm)[side])

    def w_hop(way, step, part):
        k, rows = part // 2, pl.ds((part % 2) * 32, 32)
        src = wbuf.at[0, 7, k, rows] if step == 1 else wbuf.at[way, step - 2, k, rows]
        dst = wbuf.at[1, 7, k, rows] if step == 8 else wbuf.at[way, step - 1, k, rows]
        return rcopy(src, dst, s_w.at[way, step - 1, part], r_w.at[way, step - 1, part], (zm, zp)[way])

    def carried(way, step, part):
        return step < 8 or part // 2 == 1 - way

    live_in.wait()
    block = lax.broadcasted_iota(jnp.int32, (1, 512), 1) // 64
    col = []
    for k in range(2):
        line = jnp.zeros((1, 512), F32)
        for n in range(8):
            line = jnp.where(block == n, live[k, c_index * 8 + n].astype(F32), line)
        col.append(line)

    def mask_chunk(n):
        a_in[n].wait()
        for i in (2 * n, 2 * n + 1):
            both = jnp.transpose(raw[i], (1, 0, 2))
            row = live[i, t_index].astype(F32)
            for k in range(2):
                aown[k, i * 64:(i + 1) * 64] = both[k] * (col[k] * row).astype(BF16)

    mask_chunk(0)
    mask_chunk(2)
    w_in.wait()
    pl.semaphore_wait(barrier, 7)
    for part in range(4):
        for way in range(2):
            w_hop(way, 1, part).start()
    a_own(0, 0).start()
    a_own(1, 2).start()
    mask_chunk(1)
    mask_chunk(3)
    for order in range(1, 4):
        a_own(0, order).start()
        a_own(1, (order + 2) % 4).start()

    def c_copy(t):
        return rcopy(csend.at[t], crecv.at[t], s_c.at[t], r_c.at[t], mate)

    def y1_copy(t, n):
        return rcopy(y1send.at[t, n], y1recv.at[t, n], s_y1.at[t, n], r_y1.at[t, n],
                     (ynear, yfar)[t % 2])

    def y2_copy(t):
        return rcopy(y2send.at[t], y2recv.at[t], s_y2.at[t], r_y2.at[t], (yfar, ynear)[t % 2])

    def compute(t):
        h = t % 2
        blocks = aown if t < 2 else abuf.at[t // 2 - 1]

        def pair(p, carry):
            total = jnp.zeros((512, 256), F32)
            for k in range(2):
                mine = wbuf[q, h * 4:h * 4 + 4, k].reshape(256, 512)
                theirs = wbuf[1 - q, h * 4:h * 4 + 4, k].reshape(256, 512)
                rows = jnp.concatenate([mine, theirs], axis=0)
                total = total + dot_nt(rows, blocks[k, pl.ds(pl.multiple_of(p * 256, 256), 256)])
            for n in range(2):
                cols = total[:, n * 128:(n + 1) * 128]
                kept[t, p * 2 + n] = cols[:256]
                csend[t, p * 2 + n] = cols[256:].astype(BF16)
            return carry

        lax.fori_loop(0, 2, pair, 0)
        c_copy(t).start()

    def core_sum(t):
        near, far = (yn1, yn3) if t % 2 == 0 else (yn3, yn1)
        c_copy(t).wait_recv()
        y1send[t, 1] = (kept[t, yop] + crecv[t, yop].astype(F32)).astype(BF16)
        y1_copy(t, 1).start()
        y1send[t, 0] = (kept[t, near] + crecv[t, near].astype(F32)).astype(BF16)
        y1_copy(t, 0).start()
        kept[t, far] = kept[t, far] + crecv[t, far].astype(F32)
        kept[t, y] = kept[t, y] + crecv[t, y].astype(F32)

    def y_sum1(t):
        far = (yn3, yn1)[t % 2]
        y1_copy(t, 1).wait_recv()
        y2send[t] = (kept[t, far] + y1recv[t, 1].astype(F32)).astype(BF16)
        y2_copy(t).start()

    def off(slot):
        return (1 - q) * ((slot + 1) % 8) + q * (15 - slot)

    def p_copy(t, s, i):
        return rcopy(psend.at[t, s, i], pieces.at[t // 2, z], s_p.at[t, s, i], r_p.at[t // 2, z],
                     dev(x, y, (z + off((t % 2) * 4 + s)) % NZ, i))

    low = lax.broadcasted_iota(jnp.int32, (32, 128), 1) < 64

    def y_sum2(t):
        y1_copy(t, 0).wait_recv()
        y2_copy(t).wait_recv()
        for s in range(4):
            rows = slice(s * 64, (s + 1) * 64)
            full = kept[t, y, rows] + y1recv[t, 0, rows].astype(F32) + y2recv[t, rows].astype(F32)
            top, bottom = full[:32], full[32:]
            psend[t, s, 0] = jnp.where(low, top, pltpu.roll(bottom, 64, 1)).astype(BF16)
            psend[t, s, 1] = jnp.where(low, pltpu.roll(top, 64, 1), bottom).astype(BF16)
        for s in range(4):
            p_copy(t, s, 1).start()
            if t % 2 == 1 and s == 3:
                @pl.when(q == 0)
                def _():
                    pieces[t // 2, z] = psend[t, s, 0]

                @pl.when(q != 0)
                def _():
                    p_copy(t, s, 0).start()
            else:
                p_copy(t, s, 0).start()

    def ring(step):
        for part in range(4):
            for way in range(2):
                w_hop(way, step - 1, part).wait_recv()
                if carried(way, step, part):
                    w_hop(way, step, part).start()

    def forward(first):
        for side in range(2):
            chunk = first + 2 * side
            a_own(side, chunk).wait_recv()
            a_fwd(side, chunk).start()

    ring(2)
    ring(3)
    forward(0)
    ring(4)
    ring(5)
    compute(0)
    forward(1)
    ring(6)
    core_sum(0)
    ring(7)
    y_sum1(0)
    ring(8)
    for part in range(2):
        w_hop(0, 8, part + 2).wait_recv()
        w_hop(1, 8, part).wait_recv()
    compute(1)
    a_own(0, 2).wait_recv()
    a_own(0, 3).wait_recv()
    compute(2)
    core_sum(1)
    y_sum2(0)
    compute(3)
    core_sum(2)
    a_own(1, 0).wait_recv()
    a_own(1, 1).wait_recv()
    compute(4)
    core_sum(3)
    compute(5)
    core_sum(4)
    y_sum1(1)
    core_sum(5)
    y_sum1(2)
    y_sum1(3)
    y_sum2(1)
    y_sum1(4)
    for chunk in range(4):
        a_fwd(chunk // 2, chunk).wait_recv()
    compute(6)
    y_sum1(5)
    y_sum2(2)
    compute(7)
    core_sum(6)
    y_sum2(3)
    core_sum(7)
    y_sum2(4)
    y_sum2(5)
    y_sum1(6)
    y_sum1(7)
    y_sum2(6)
    y_sum2(7)

    for stage in range(4):
        xs = (x + (0, 3, 1, 2)[stage]) % 4

        def arrive(n, carry):
            @pl.when((n != z) | (q != 0))
            def _():
                rcopy(psend.at[0, 0, 0], pieces.at[stage, n], s_p.at[0, 0, 0], r_p.at[stage, n],
                      mate).wait_recv()

            return carry

        lax.fori_loop(0, NZ, arrive, 0)
        for m in range(NZ // 2):
            even, odd = pieces[stage, 2 * m].astype(F32), pieces[stage, 2 * m + 1].astype(F32)
            cols = pl.ds(pl.multiple_of(xs * 1024 + m * 128, 128), 128)
            out_ref[0:32, cols] = jnp.where(low, even, pltpu.roll(odd, 64, 1)).astype(BF16)
            out_ref[32:64, cols] = jnp.where(low, pltpu.roll(even, 64, 1), odd).astype(BF16)

    for way in range(2):
        for n in range(1, 9):
            for part in range(4):
                if carried(way, n, part):
                    w_hop(way, n, part).wait_send()
        for chunk in range(4):
            a_own(way, chunk).wait_send()
    for chunk in range(4):
        a_fwd(chunk // 2, chunk).wait_send()
    for t in range(8):
        c_copy(t).wait_send()
        y1_copy(t, 0).wait_send()
        y1_copy(t, 1).wait_send()
        y2_copy(t).wait_send()
        for s in range(4):
            p_copy(t, s, 1).wait_send()
            if t % 2 == 1 and s == 3:
                @pl.when(q != 0)
                def _():
                    p_copy(t, s, 0).wait_send()
            else:
                p_copy(t, s, 0).wait_send()


def fused(amplitudes, tiles, pair_live):
    dma = pltpu.SemaphoreType.DMA
    return pl.pallas_call(
        kernel,
        out_shape=jax.ShapeDtypeStruct((64, 4096), BF16),
        in_specs=[pl.BlockSpec(memory_space=pl.ANY)] * 3,
        out_specs=pl.BlockSpec(memory_space=pltpu.VMEM),
        scratch_shapes=[
            pltpu.VMEM((8, 64, 2, 512), BF16),
            pltpu.SMEM((8, 64), jnp.int32),
            pltpu.VMEM((2, 512, 512), BF16),
            pltpu.VMEM((3, 2, 512, 512), BF16),
            pltpu.VMEM((2, 8, 2, 64, 512), BF16),
            pltpu.VMEM((8, 4, 256, 128), F32),
            pltpu.VMEM((8, 4, 256, 128), BF16),
            pltpu.VMEM((8, 4, 256, 128), BF16),
            pltpu.VMEM((8, 2, 256, 128), BF16),
            pltpu.VMEM((8, 2, 256, 128), BF16),
            pltpu.VMEM((8, 256, 128), BF16),
            pltpu.VMEM((8, 256, 128), BF16),
            pltpu.VMEM((8, 4, 2, 32, 128), BF16),
            pltpu.VMEM((4, NZ, 32, 128), BF16),
            dma((6,)), dma((2, 4)), dma((4,)), dma((3, 4)),
            dma((2, 8, 4)), dma((2, 8, 4)),
            dma((8,)), dma((8,)), dma((8, 2)), dma((8, 2)), dma((8,)), dma((8,)),
            dma((8, 4, 2)), dma((4, NZ)),
        ],
        compiler_params=pltpu.CompilerParams(
            collective_id=0, has_side_effects=True, vmem_limit_bytes=56 * 1024 * 1024
        ),
        name="cycle_fused",
    )(amplitudes, tiles, pair_live)


def per_device(amplitudes, cycle_integrals, pair_live):
    tiles = cycle_integrals[:, :, 0, :].transpose(0, 2, 1)
    return fused(amplitudes, tiles, pair_live).reshape(1, 64, 1, 4096)


def solution(mesh):
    return jax.shard_map(
        per_device,
        mesh=mesh,
        in_specs=(P(None, "tr", None, "ct"), P(None, "ct", None, "tr"), P()),
        out_specs=P("ct", "tr", None, None),
        check_vma=False,
    )
```

```python
import functools

import jax
import jax.numpy as jnp
from jax import lax
from jax.experimental import pallas as pl
from jax.experimental.pallas import tpu as pltpu
from jax.sharding import PartitionSpec as P

MESH = pl.DeviceIdType.MESH
F32 = jnp.float32
BF16 = jnp.bfloat16
NZ = 16
GROUPS = ((0, 4), (4, 6), (6, 8))
UNITS = [(stage, group) for stage in range(4) for group in range(3)]


def dot_nt(lhs, rhs):
    return lax.dot_general(lhs, rhs, (((1,), (1,)), ((), ())), preferred_element_type=F32)


def kernel(
    a_hbm, w_hbm, live_hbm, out_ref,
    raw, live, aown, abuf, wbuf, kept, csend, crecv, y1send, y1recv, y2send, y2recv, psend, pieces, relay,
    s_in, s_a, s_af, r_a, s_w, r_w, s_c, r_c, s_y1, r_y1, s_y2, r_y2, s_p, r_p, s_relay, r_relay,
):
    t_index = lax.axis_index("tr")
    c_index = lax.axis_index("ct")
    x, z = t_index // NZ, t_index % NZ
    y, q = c_index // 2, c_index % 2
    yn1 = y + 1 - 2 * (y % 2)
    yn3 = 3 - y
    yop = (y + 2) % 4

    def dev(xx, yy, zz, qq):
        return (xx * NZ + zz, yy * 2 + qq)

    xp, xm = dev((x + 1) % 4, y, z, q), dev((x + 3) % 4, y, z, q)
    zp, zm = dev(x, y, (z + 1) % NZ, q), dev(x, y, (z + NZ - 1) % NZ, q)
    mate = dev(x, y, z, 1 - q)
    ynear, yfar = dev(x, yn1, z, q), dev(x, yn3, z, q)

    def rcopy(src, dst, ssem, rsem, to):
        return pltpu.make_async_remote_copy(
            src_ref=src, dst_ref=dst, send_sem=ssem, recv_sem=rsem, device_id=to, device_id_type=MESH
        )

    barrier = pltpu.get_barrier_semaphore()
    for other in (zp, zm, xp, xm, mate, ynear, yfar):
        pl.semaphore_signal(barrier, inc=1, device_id=other, device_id_type=MESH)

    live_in = pltpu.make_async_copy(live_hbm, live, s_in.at[0])
    w_in = pltpu.make_async_copy(w_hbm, wbuf.at[0, 7], s_in.at[1])
    a_in = [
        pltpu.make_async_copy(a_hbm.at[pl.ds(2 * n, 2)], raw.at[pl.ds(2 * n, 2)], s_in.at[2 + n])
        for n in range(4)
    ]
    live_in.start()
    for n in (0, 2, 1, 3):
        a_in[n].start()
    w_in.start()

    def a_own(side, chunk):
        rows = pl.ds(chunk * 128, 128)
        return rcopy(aown.at[:, rows], abuf.at[side, :, rows], s_a.at[side, chunk], r_a.at[side, chunk],
                     (xp, xm)[side])

    def a_fwd(side, chunk):
        rows = pl.ds(chunk * 128, 128)
        return rcopy(abuf.at[side, :, rows], abuf.at[2, :, rows], s_af.at[chunk], r_a.at[2, chunk],
                     (xp, xm)[side])

    def w_hop(way, step, part):
        k, rows = part // 2, pl.ds((part % 2) * 32, 32)
        src = wbuf.at[0, 7, k, rows] if step == 1 else wbuf.at[way, step - 2, k, rows]
        dst = wbuf.at[1, 7, k, rows] if step == 8 else wbuf.at[way, step - 1, k, rows]
        return rcopy(src, dst, s_w.at[way, step - 1, part], r_w.at[way, step - 1, part], (zm, zp)[way])

    def carried(way, step, part):
        return step < 8 or part // 2 == 1 - way

    live_in.wait()
    block = lax.broadcasted_iota(jnp.int32, (1, 512), 1) // 64
    col = []
    for k in range(2):
        line = jnp.zeros((1, 512), F32)
        for n in range(8):
            line = jnp.where(block == n, live[k, c_index * 8 + n].astype(F32), line)
        col.append(line)

    def mask_chunk(n):
        a_in[n].wait()
        for i in (2 * n, 2 * n + 1):
            both = jnp.transpose(raw[i], (1, 0, 2))
            row = live[i, t_index].astype(F32)
            for k in range(2):
                aown[k, i * 64:(i + 1) * 64] = both[k] * (col[k] * row).astype(BF16)

    mask_chunk(0)
    mask_chunk(2)
    w_in.wait()
    pl.semaphore_wait(barrier, 7)
    for part in range(4):
        for way in range(2):
            w_hop(way, 1, part).start()
    a_own(0, 0).start()
    a_own(1, 2).start()
    mask_chunk(1)
    mask_chunk(3)
    for order in range(1, 4):
        a_own(0, order).start()
        a_own(1, (order + 2) % 4).start()

    def rows_of(n):
        lo, hi = GROUPS[UNITS[n][1]]
        return pl.ds(lo * 64, (hi - lo) * 64)

    def swapped(n):
        stage, group = UNITS[n]
        return (stage + (group > 0)) % 2

    def c_copy(n):
        part = (UNITS[n][0], slice(None), rows_of(n))
        return rcopy(csend.at[part], crecv.at[part], s_c.at[n], r_c.at[n], mate)

    def y1_copy(n, b):
        part = (UNITS[n][0], b, rows_of(n))
        return rcopy(y1send.at[part], y1recv.at[part], s_y1.at[n, b], r_y1.at[n, b],
                     (ynear, yfar)[swapped(n)])

    def y2_copy(n):
        part = (UNITS[n][0], rows_of(n))
        return rcopy(y2send.at[part], y2recv.at[part], s_y2.at[n], r_y2.at[n],
                     (yfar, ynear)[swapped(n)])

    def compute(n):
        stage, group = UNITS[n]
        lo, hi = GROUPS[group]
        size = (hi - lo) * 64
        blocks = abuf.at[stage - 1] if stage else aown

        def pair(p, carry):
            total = jnp.zeros((2 * size, 256), F32)
            for k in range(2):
                mine = wbuf[q, lo:hi, k].reshape(size, 512)
                theirs = wbuf[1 - q, lo:hi, k].reshape(size, 512)
                rows = jnp.concatenate([mine, theirs], axis=0)
                total = total + dot_nt(rows, blocks[k, pl.ds(pl.multiple_of(p * 256, 256), 256)])
            for b in range(2):
                cols = total[:, b * 128:(b + 1) * 128]
                kept[stage, p * 2 + b, rows_of(n)] = cols[:size]
                csend[stage, p * 2 + b, rows_of(n)] = cols[size:].astype(BF16)
            return carry

        lax.fori_loop(0, 2, pair, 0)
        c_copy(n).start()

    def core_sum(n):
        stage, rows = UNITS[n][0], rows_of(n)
        near, far = (yn3, yn1) if swapped(n) else (yn1, yn3)
        c_copy(n).wait_recv()
        y1send[stage, 1, rows] = (kept[stage, yop, rows] + crecv[stage, yop, rows].astype(F32)).astype(BF16)
        y1_copy(n, 1).start()
        y1send[stage, 0, rows] = (kept[stage, near, rows] + crecv[stage, near, rows].astype(F32)).astype(BF16)
        y1_copy(n, 0).start()
        kept[stage, far, rows] = kept[stage, far, rows] + crecv[stage, far, rows].astype(F32)
        kept[stage, y, rows] = kept[stage, y, rows] + crecv[stage, y, rows].astype(F32)

    def y_sum1(n):
        stage, rows = UNITS[n][0], rows_of(n)
        far = yn1 if swapped(n) else yn3
        y1_copy(n, 1).wait_recv()
        y2send[stage, rows] = (kept[stage, far, rows] + y1recv[stage, 1, rows].astype(F32)).astype(BF16)
        y2_copy(n).start()

    def off(slot):
        return (1 - q) * ((slot + 1) % 8) + q * (15 - slot)

    def p_copy(stage, slot, i):
        return rcopy(psend.at[stage, slot, i], pieces.at[stage, z], s_p.at[stage, slot, i],
                     r_p.at[stage, z], dev(x, y, (z + off(slot)) % NZ, i))

    def half_way(stage, i):
        return rcopy(psend.at[stage, 7, i], relay.at[stage, i], s_p.at[stage, 7, i],
                     r_relay.at[stage, i], dev(x, y, (z + 12) % NZ, q))

    def other_half(stage, i):
        origin = (z + 4) % NZ
        return rcopy(relay.at[stage, i], pieces.at[stage, origin], s_relay.at[stage, i],
                     r_p.at[stage, origin], dev(x, y, (z + 12) % NZ, i))

    def relay_on(stage):
        @pl.when(q != 0)
        def _():
            for i in range(2):
                half_way(stage, i).wait_recv()
                other_half(stage, i).start()

    low = lax.broadcasted_iota(jnp.int32, (32, 128), 1) < 64

    def last_slot(stage, own, away):
        @pl.when(q == 0)
        def _():
            own()

        @pl.when(q != 0)
        def _():
            for i in range(2):
                away(half_way(stage, i) if stage < 2 else p_copy(stage, 7, i))

    def y_sum2(n):
        stage, group = UNITS[n]
        lo, hi = GROUPS[group]
        y1_copy(n, 0).wait_recv()
        y2_copy(n).wait_recv()
        for slot in range(lo, hi):
            rows = slice(slot * 64, (slot + 1) * 64)
            full = (kept[stage, y, rows] + y1recv[stage, 0, rows].astype(F32)
                    + y2recv[stage, rows].astype(F32))
            top, bottom = full[:32], full[32:]
            psend[stage, slot, 0] = jnp.where(low, top, pltpu.roll(bottom, 64, 1)).astype(BF16)
            psend[stage, slot, 1] = jnp.where(low, pltpu.roll(top, 64, 1), bottom).astype(BF16)
        for slot in range(hi - 1, lo - 1, -1):
            if slot < 7:
                p_copy(stage, slot, 0).start()
                p_copy(stage, slot, 1).start()
            else:
                def own():
                    pieces[stage, z] = psend[stage, 7, 0]
                    p_copy(stage, 7, 1).start()

                last_slot(stage, own, lambda copy: copy.start())

    def ring(step):
        for part in range(4):
            for way in range(2):
                w_hop(way, step - 1, part).wait_recv()
                if carried(way, step, part):
                    w_hop(way, step, part).start()

    def forward(first):
        for side in range(2):
            chunk = first + 2 * side
            a_own(side, chunk).wait_recv()
            a_fwd(side, chunk).start()

    ring(2)
    ring(3)
    ring(4)
    ring(5)
    compute(0)
    ring(6)
    forward(0)
    forward(1)
    core_sum(0)
    ring(7)
    y_sum1(0)
    compute(1)
    ring(8)
    core_sum(1)
    y_sum2(0)
    a_own(1, 0).wait_recv()
    a_own(1, 1).wait_recv()
    a_own(0, 2).wait_recv()
    a_own(0, 3).wait_recv()
    compute(7)
    for part in range(2):
        w_hop(0, 8, part + 2).wait_recv()
        w_hop(1, 8, part).wait_recv()
    compute(4)
    compute(3)
    y_sum1(1)
    core_sum(7)
    compute(2)
    core_sum(4)
    compute(5)
    compute(8)
    core_sum(2)
    y_sum1(7)
    core_sum(5)
    compute(6)
    core_sum(8)
    y_sum2(1)
    y_sum1(4)
    y_sum1(2)
    core_sum(6)
    y_sum2(7)
    for chunk in range(4):
        a_fwd(chunk // 2, chunk).wait_recv()
    y_sum1(5)
    compute(11)
    core_sum(3)
    y_sum1(8)
    y_sum2(2)
    y_sum2(4)
    core_sum(11)
    y_sum2(5)
    y_sum1(6)
    compute(9)
    y_sum1(3)
    y_sum2(8)
    compute(10)
    y_sum1(11)
    core_sum(9)
    core_sum(10)
    y_sum2(6)
    y_sum2(3)
    y_sum1(10)
    y_sum1(9)
    relay_on(1)
    y_sum2(11)
    relay_on(0)
    y_sum2(10)
    y_sum2(9)

    for stage in range(4):
        xs = (x + (0, 3, 1, 2)[stage]) % 4

        def arrive(n, carry):
            @pl.when((n != z) | (q != 0))
            def _():
                rcopy(psend.at[0, 0, 0], pieces.at[stage, n], s_p.at[0, 0, 0], r_p.at[stage, n],
                      mate).wait_recv()

            return carry

        lax.fori_loop(0, NZ, arrive, 0)
        for m in range(NZ // 2):
            even, odd = pieces[stage, 2 * m].astype(F32), pieces[stage, 2 * m + 1].astype(F32)
            cols = pl.ds(pl.multiple_of(xs * 1024 + m * 128, 128), 128)
            out_ref[0:32, cols] = jnp.where(low, even, pltpu.roll(odd, 64, 1)).astype(BF16)
            out_ref[32:64, cols] = jnp.where(low, pltpu.roll(even, 64, 1), odd).astype(BF16)

    for way in range(2):
        for n in range(1, 9):
            for part in range(4):
                if carried(way, n, part):
                    w_hop(way, n, part).wait_send()
        for chunk in range(4):
            a_own(way, chunk).wait_send()
    for chunk in range(4):
        a_fwd(chunk // 2, chunk).wait_send()
    for n in range(len(UNITS)):
        c_copy(n).wait_send()
        y1_copy(n, 0).wait_send()
        y1_copy(n, 1).wait_send()
        y2_copy(n).wait_send()
    for stage in range(4):
        for slot in range(7):
            p_copy(stage, slot, 0).wait_send()
            p_copy(stage, slot, 1).wait_send()
        last_slot(stage, lambda: p_copy(stage, 7, 1).wait_send(), lambda copy: copy.wait_send())

    @pl.when(q != 0)
    def _():
        for stage in range(2):
            for i in range(2):
                other_half(stage, i).wait_send()


def fused(amplitudes, tiles, pair_live):
    dma = pltpu.SemaphoreType.DMA
    return pl.pallas_call(
        kernel,
        out_shape=jax.ShapeDtypeStruct((64, 4096), BF16),
        in_specs=[pl.BlockSpec(memory_space=pl.ANY)] * 3,
        out_specs=pl.BlockSpec(memory_space=pltpu.VMEM),
        scratch_shapes=[
            pltpu.VMEM((8, 64, 2, 512), BF16),
            pltpu.SMEM((8, 64), jnp.int32),
            pltpu.VMEM((2, 512, 512), BF16),
            pltpu.VMEM((3, 2, 512, 512), BF16),
            pltpu.VMEM((2, 8, 2, 64, 512), BF16),
            pltpu.VMEM((4, 4, 512, 128), F32),
            pltpu.VMEM((4, 4, 512, 128), BF16),
            pltpu.VMEM((4, 4, 512, 128), BF16),
            pltpu.VMEM((4, 2, 512, 128), BF16),
            pltpu.VMEM((4, 2, 512, 128), BF16),
            pltpu.VMEM((4, 512, 128), BF16),
            pltpu.VMEM((4, 512, 128), BF16),
            pltpu.VMEM((4, 8, 2, 32, 128), BF16),
            pltpu.VMEM((4, NZ, 32, 128), BF16),
            pltpu.VMEM((2, 2, 32, 128), BF16),
            dma((6,)), dma((2, 4)), dma((4,)), dma((3, 4)),
            dma((2, 8, 4)), dma((2, 8, 4)),
            dma((12,)), dma((12,)), dma((12, 2)), dma((12, 2)), dma((12,)), dma((12,)),
            dma((4, 8, 2)), dma((4, NZ)), dma((2, 2)), dma((2, 2)),
        ],
        compiler_params=pltpu.CompilerParams(
            collective_id=0, has_side_effects=True, vmem_limit_bytes=56 * 1024 * 1024
        ),
        name="cycle_fused",
    )(amplitudes, tiles, pair_live)


def per_device(amplitudes, cycle_integrals, pair_live):
    tiles = cycle_integrals[:, :, 0, :].transpose(0, 2, 1)
    return fused(amplitudes, tiles, pair_live).reshape(1, 64, 1, 4096)


def solution(mesh):
    return jax.shard_map(
        per_device,
        mesh=mesh,
        in_specs=(P(None, "tr", None, "ct"), P(None, "ct", None, "tr"), P()),
        out_specs=P("ct", "tr", None, None),
        check_vma=False,
    )
```

```python
import functools

import jax
import jax.numpy as jnp
from jax import lax
from jax.experimental import pallas as pl
from jax.experimental.pallas import tpu as pltpu
from jax.sharding import PartitionSpec as P

MESH = pl.DeviceIdType.MESH
F32 = jnp.float32
BF16 = jnp.bfloat16
NZ = 16
GROUPS = ((0, 4), (4, 6), (6, 8))
UNITS = [(stage, group) for stage in range(4) for group in range(3)]


def dot_nt(lhs, rhs):
    return lax.dot_general(lhs, rhs, (((1,), (1,)), ((), ())), preferred_element_type=F32)


def kernel(
    a_hbm, w_hbm, live_hbm, out_ref,
    raw, live, aown, abuf, wbuf, kept, csend, crecv, y1send, y1recv, y2send, y2recv, psend, pieces, relay,
    s_in, s_a, s_af, r_a, s_w, r_w, s_c, r_c, s_y1, r_y1, s_y2, r_y2, s_p, r_p, s_relay, r_relay,
):
    t_index = lax.axis_index("tr")
    c_index = lax.axis_index("ct")
    x, z = t_index // NZ, t_index % NZ
    y, q = c_index // 2, c_index % 2
    yn1 = y + 1 - 2 * (y % 2)
    yn3 = 3 - y
    yop = (y + 2) % 4

    def dev(xx, yy, zz, qq):
        return (xx * NZ + zz, yy * 2 + qq)

    xp, xm = dev((x + 1) % 4, y, z, q), dev((x + 3) % 4, y, z, q)
    zp, zm = dev(x, y, (z + 1) % NZ, q), dev(x, y, (z + NZ - 1) % NZ, q)
    mate = dev(x, y, z, 1 - q)
    ynear, yfar = dev(x, yn1, z, q), dev(x, yn3, z, q)

    def rcopy(src, dst, ssem, rsem, to):
        return pltpu.make_async_remote_copy(
            src_ref=src, dst_ref=dst, send_sem=ssem, recv_sem=rsem, device_id=to, device_id_type=MESH
        )

    barrier = pltpu.get_barrier_semaphore()
    for other in (zp, zm, xp, xm, mate, ynear, yfar):
        pl.semaphore_signal(barrier, inc=1, device_id=other, device_id_type=MESH)

    live_in = pltpu.make_async_copy(live_hbm, live, s_in.at[0])
    w_in = pltpu.make_async_copy(w_hbm, wbuf.at[0, 7], s_in.at[1])
    a_in = [
        pltpu.make_async_copy(a_hbm.at[pl.ds(2 * n, 2)], raw.at[pl.ds(2 * n, 2)], s_in.at[2 + n])
        for n in range(4)
    ]
    live_in.start()
    for n in (0, 2, 1, 3):
        a_in[n].start()
    w_in.start()

    def a_own(side, chunk):
        rows = pl.ds(chunk * 128, 128)
        return rcopy(aown.at[:, rows], abuf.at[side, :, rows], s_a.at[side, chunk], r_a.at[side, chunk],
                     (xp, xm)[side])

    def a_fwd(side, chunk):
        rows = pl.ds(chunk * 128, 128)
        return rcopy(abuf.at[side, :, rows], abuf.at[2, :, rows], s_af.at[chunk], r_a.at[2, chunk],
                     (xp, xm)[side])

    def w_hop(way, step, part):
        k, rows = part // 2, pl.ds((part % 2) * 32, 32)
        src = wbuf.at[0, 7, k, rows] if step == 1 else wbuf.at[way, step - 2, k, rows]
        dst = wbuf.at[1, 7, k, rows] if step == 8 else wbuf.at[way, step - 1, k, rows]
        return rcopy(src, dst, s_w.at[way, step - 1, part], r_w.at[way, step - 1, part], (zm, zp)[way])

    def carried(way, step, part):
        return step < 8 or part // 2 == 1 - way

    live_in.wait()
    block = lax.broadcasted_iota(jnp.int32, (1, 512), 1) // 64
    col = []
    for k in range(2):
        line = jnp.zeros((1, 512), F32)
        for n in range(8):
            line = jnp.where(block == n, live[k, c_index * 8 + n].astype(F32), line)
        col.append(line)

    def mask_chunk(n):
        a_in[n].wait()
        for i in (2 * n, 2 * n + 1):
            both = jnp.transpose(raw[i], (1, 0, 2))
            row = live[i, t_index].astype(F32)
            for k in range(2):
                aown[k, i * 64:(i + 1) * 64] = both[k] * (col[k] * row).astype(BF16)

    mask_chunk(0)
    mask_chunk(2)
    w_in.wait()
    pl.semaphore_wait(barrier, 7)
    for part in range(4):
        for way in range(2):
            w_hop(way, 1, part).start()
    a_own(0, 0).start()
    a_own(1, 2).start()
    mask_chunk(1)
    mask_chunk(3)
    for order in range(1, 4):
        a_own(0, order).start()
        a_own(1, (order + 2) % 4).start()

    def rows_of(n):
        lo, hi = GROUPS[UNITS[n][1]]
        return pl.ds(lo * 64, (hi - lo) * 64)

    def swapped(n):
        stage, group = UNITS[n]
        return (stage + (group > 0)) % 2

    def c_copy(n):
        part = (UNITS[n][0], slice(None), rows_of(n))
        return rcopy(csend.at[part], crecv.at[part], s_c.at[n], r_c.at[n], mate)

    def y1_copy(n, b):
        part = (UNITS[n][0], b, rows_of(n))
        return rcopy(y1send.at[part], y1recv.at[part], s_y1.at[n, b], r_y1.at[n, b],
                     (ynear, yfar)[swapped(n)])

    def y2_copy(n):
        part = (UNITS[n][0], rows_of(n))
        return rcopy(y2send.at[part], y2recv.at[part], s_y2.at[n], r_y2.at[n],
                     (yfar, ynear)[swapped(n)])

    def compute(n):
        stage, group = UNITS[n]
        lo, hi = GROUPS[group]
        size = (hi - lo) * 64
        blocks = abuf.at[stage - 1] if stage else aown

        def pair(p, carry):
            total = jnp.zeros((2 * size, 256), F32)
            for k in range(2):
                mine = wbuf[q, lo:hi, k].reshape(size, 512)
                theirs = wbuf[1 - q, lo:hi, k].reshape(size, 512)
                rows = jnp.concatenate([mine, theirs], axis=0)
                total = total + dot_nt(rows, blocks[k, pl.ds(pl.multiple_of(p * 256, 256), 256)])
            for b in range(2):
                cols = total[:, b * 128:(b + 1) * 128]
                kept[stage, p * 2 + b, rows_of(n)] = cols[:size]
                csend[stage, p * 2 + b, rows_of(n)] = cols[size:].astype(BF16)
            return carry

        lax.fori_loop(0, 2, pair, 0)
        c_copy(n).start()

    def core_sum(n):
        stage, rows = UNITS[n][0], rows_of(n)
        near, far = (yn3, yn1) if swapped(n) else (yn1, yn3)
        c_copy(n).wait_recv()
        y1send[stage, 1, rows] = (kept[stage, yop, rows] + crecv[stage, yop, rows].astype(F32)).astype(BF16)
        y1_copy(n, 1).start()
        y1send[stage, 0, rows] = (kept[stage, near, rows] + crecv[stage, near, rows].astype(F32)).astype(BF16)
        y1_copy(n, 0).start()
        kept[stage, far, rows] = kept[stage, far, rows] + crecv[stage, far, rows].astype(F32)
        kept[stage, y, rows] = kept[stage, y, rows] + crecv[stage, y, rows].astype(F32)

    def y_sum1(n):
        stage, rows = UNITS[n][0], rows_of(n)
        far = yn1 if swapped(n) else yn3
        y1_copy(n, 1).wait_recv()
        y2send[stage, rows] = (kept[stage, far, rows] + y1recv[stage, 1, rows].astype(F32)).astype(BF16)
        y2_copy(n).start()

    def off(slot):
        return (1 - q) * ((slot + 1) % 8) + q * (15 - slot)

    def p_copy(stage, slot, i):
        return rcopy(psend.at[stage, slot, i], pieces.at[stage, z], s_p.at[stage, slot, i],
                     r_p.at[stage, z], dev(x, y, (z + off(slot)) % NZ, i))

    def half_way(stage, i):
        return rcopy(psend.at[stage, 7, i], relay.at[stage, i], s_p.at[stage, 7, i],
                     r_relay.at[stage, i], dev(x, y, (z + 12) % NZ, q))

    def other_half(stage, i):
        origin = (z + 4) % NZ
        return rcopy(relay.at[stage, i], pieces.at[stage, origin], s_relay.at[stage, i],
                     r_p.at[stage, origin], dev(x, y, (z + 12) % NZ, i))

    def relay_on(stage):
        @pl.when(q != 0)
        def _():
            for i in range(2):
                half_way(stage, i).wait_recv()
                other_half(stage, i).start()

    low = lax.broadcasted_iota(jnp.int32, (32, 128), 1) < 64

    def last_slot(stage, own, away):
        @pl.when(q == 0)
        def _():
            own()

        @pl.when(q != 0)
        def _():
            for i in range(2):
                away(half_way(stage, i) if stage < 2 else p_copy(stage, 7, i))

    def y_sum2(n):
        stage, group = UNITS[n]
        lo, hi = GROUPS[group]
        y1_copy(n, 0).wait_recv()
        y2_copy(n).wait_recv()
        for slot in range(lo, hi):
            rows = slice(slot * 64, (slot + 1) * 64)
            full = (kept[stage, y, rows] + y1recv[stage, 0, rows].astype(F32)
                    + y2recv[stage, rows].astype(F32))
            top, bottom = full[:32], full[32:]
            psend[stage, slot, 0] = jnp.where(low, top, pltpu.roll(bottom, 64, 1)).astype(BF16)
            psend[stage, slot, 1] = jnp.where(low, pltpu.roll(top, 64, 1), bottom).astype(BF16)
        for slot in range(hi - 1, lo - 1, -1):
            if slot < 7:
                p_copy(stage, slot, 0).start()
                p_copy(stage, slot, 1).start()
            else:
                def own():
                    pieces[stage, z] = psend[stage, 7, 0]
                    p_copy(stage, 7, 1).start()

                last_slot(stage, own, lambda copy: copy.start())

    def ring(step):
        for part in range(4):
            for way in range(2):
                w_hop(way, step - 1, part).wait_recv()
                if carried(way, step, part):
                    w_hop(way, step, part).start()

    def forward(first):
        for side in range(2):
            chunk = first + 2 * side
            a_own(side, chunk).wait_recv()
            a_fwd(side, chunk).start()

    ring(2)
    ring(3)
    ring(4)
    ring(5)
    compute(0)
    ring(6)
    forward(0)
    forward(1)
    core_sum(0)
    ring(7)
    y_sum1(0)
    compute(1)
    ring(8)
    core_sum(1)
    y_sum2(0)
    a_own(1, 0).wait_recv()
    a_own(1, 1).wait_recv()
    a_own(0, 2).wait_recv()
    a_own(0, 3).wait_recv()
    compute(7)
    for part in range(2):
        w_hop(0, 8, part + 2).wait_recv()
        w_hop(1, 8, part).wait_recv()
    compute(4)
    compute(3)
    y_sum1(1)
    core_sum(7)
    compute(2)
    core_sum(4)
    compute(5)
    compute(8)
    core_sum(2)
    y_sum1(7)
    core_sum(5)
    compute(6)
    core_sum(8)
    y_sum2(1)
    y_sum1(4)
    y_sum1(2)
    core_sum(6)
    y_sum2(7)
    for chunk in range(4):
        a_fwd(chunk // 2, chunk).wait_recv()
    y_sum1(5)
    compute(11)
    core_sum(3)
    y_sum1(8)
    y_sum2(2)
    y_sum2(4)
    core_sum(11)
    y_sum2(5)
    y_sum1(6)
    compute(9)
    y_sum1(3)
    y_sum2(8)
    compute(10)
    y_sum1(11)
    core_sum(9)
    core_sum(10)
    y_sum2(6)
    y_sum2(3)
    y_sum1(10)
    y_sum1(9)
    relay_on(1)
    y_sum2(11)
    relay_on(0)
    y_sum2(10)
    y_sum2(9)

    for stage in range(4):
        xs = (x + (0, 3, 1, 2)[stage]) % 4

        def arrive(n, carry):
            @pl.when((n != z) | (q != 0))
            def _():
                rcopy(psend.at[0, 0, 0], pieces.at[stage, n], s_p.at[0, 0, 0], r_p.at[stage, n],
                      mate).wait_recv()

            return carry

        lax.fori_loop(0, NZ, arrive, 0)
        for m in range(NZ // 2):
            even, odd = pieces[stage, 2 * m].astype(F32), pieces[stage, 2 * m + 1].astype(F32)
            cols = pl.ds(pl.multiple_of(xs * 1024 + m * 128, 128), 128)
            out_ref[0:32, cols] = jnp.where(low, even, pltpu.roll(odd, 64, 1)).astype(BF16)
            out_ref[32:64, cols] = jnp.where(low, pltpu.roll(even, 64, 1), odd).astype(BF16)

    for way in range(2):
        for n in range(1, 9):
            for part in range(4):
                if carried(way, n, part):
                    w_hop(way, n, part).wait_send()
        for chunk in range(4):
            a_own(way, chunk).wait_send()
    for chunk in range(4):
        a_fwd(chunk // 2, chunk).wait_send()
    for n in range(len(UNITS)):
        c_copy(n).wait_send()
        y1_copy(n, 0).wait_send()
        y1_copy(n, 1).wait_send()
        y2_copy(n).wait_send()
    for stage in range(4):
        for slot in range(7):
            p_copy(stage, slot, 0).wait_send()
            p_copy(stage, slot, 1).wait_send()
        last_slot(stage, lambda: p_copy(stage, 7, 1).wait_send(), lambda copy: copy.wait_send())

    @pl.when(q != 0)
    def _():
        for stage in range(2):
            for i in range(2):
                other_half(stage, i).wait_send()


def fused(amplitudes, tiles, pair_live):
    dma = pltpu.SemaphoreType.DMA
    return pl.pallas_call(
        kernel,
        out_shape=jax.ShapeDtypeStruct((64, 4096), BF16),
        in_specs=[pl.BlockSpec(memory_space=pl.ANY)] * 3,
        out_specs=pl.BlockSpec(memory_space=pltpu.VMEM),
        scratch_shapes=[
            pltpu.VMEM((8, 64, 2, 512), BF16),
            pltpu.SMEM((8, 64), jnp.int32),
            pltpu.VMEM((2, 512, 512), BF16),
            pltpu.VMEM((3, 2, 512, 512), BF16),
            pltpu.VMEM((2, 8, 2, 64, 512), BF16),
            pltpu.VMEM((4, 4, 512, 128), F32),
            pltpu.VMEM((4, 4, 512, 128), BF16),
            pltpu.VMEM((4, 4, 512, 128), BF16),
            pltpu.VMEM((4, 2, 512, 128), BF16),
            pltpu.VMEM((4, 2, 512, 128), BF16),
            pltpu.VMEM((4, 512, 128), BF16),
            pltpu.VMEM((4, 512, 128), BF16),
            pltpu.VMEM((4, 8, 2, 32, 128), BF16),
            pltpu.VMEM((4, NZ, 32, 128), BF16),
            pltpu.VMEM((2, 2, 32, 128), BF16),
            dma((6,)), dma((2, 4)), dma((4,)), dma((3, 4)),
            dma((2, 8, 4)), dma((2, 8, 4)),
            dma((12,)), dma((12,)), dma((12, 2)), dma((12, 2)), dma((12,)), dma((12,)),
            dma((4, 8, 2)), dma((4, NZ)), dma((2, 2)), dma((2, 2)),
        ],
        compiler_params=pltpu.CompilerParams(
            collective_id=0, has_side_effects=True, vmem_limit_bytes=40 * 1024 * 1024
        ),
        name="cycle_fused",
    )(amplitudes, tiles, pair_live)


def per_device(amplitudes, cycle_integrals, pair_live):
    tiles = cycle_integrals[:, :, 0, :].transpose(0, 2, 1)
    operands = [
        pltpu.with_memory_space_constraint(operand, pltpu.HBM)
        for operand in (amplitudes, tiles, pair_live)
    ]
    return fused(*operands).reshape(1, 64, 1, 4096)


def solution(mesh):
    return jax.shard_map(
        per_device,
        mesh=mesh,
        in_specs=(P(None, "tr", None, "ct"), P(None, "ct", None, "tr"), P()),
        out_specs=P("ct", "tr", None, None),
        check_vma=False,
    )
```

```python
import functools

import jax
import jax.numpy as jnp
from jax import lax
from jax.experimental import pallas as pl
from jax.experimental.pallas import tpu as pltpu
from jax.sharding import PartitionSpec as P

MESH = pl.DeviceIdType.MESH
F32 = jnp.float32
BF16 = jnp.bfloat16
NZ = 16
GROUPS = ((0, 4), (4, 6), (6, 8))
UNITS = [(stage, group) for stage in range(4) for group in range(3)]


def dot_nt(lhs, rhs):
    return lax.dot_general(lhs, rhs, (((1,), (1,)), ((), ())), preferred_element_type=F32)


def kernel(
    a_hbm, w_hbm, live_hbm, out_ref,
    raw, live, aown, abuf, wbuf, kept, csend, crecv, y1send, y1recv, y2send, y2recv, psend, pieces, relay,
    s_in, s_a, s_af, r_a, s_w, r_w, s_c, r_c, s_y1, r_y1, s_y2, r_y2, s_p, r_p, s_relay, r_relay,
):
    t_index = lax.axis_index("tr")
    c_index = lax.axis_index("ct")
    x, z = t_index // NZ, t_index % NZ
    y, q = c_index // 2, c_index % 2
    yn1 = y + 1 - 2 * (y % 2)
    yn3 = 3 - y
    yop = (y + 2) % 4

    def dev(xx, yy, zz, qq):
        return (xx * NZ + zz, yy * 2 + qq)

    xp, xm = dev((x + 1) % 4, y, z, q), dev((x + 3) % 4, y, z, q)
    zp, zm = dev(x, y, (z + 1) % NZ, q), dev(x, y, (z + NZ - 1) % NZ, q)
    mate = dev(x, y, z, 1 - q)
    ynear, yfar = dev(x, yn1, z, q), dev(x, yn3, z, q)

    def rcopy(src, dst, ssem, rsem, to):
        return pltpu.make_async_remote_copy(
            src_ref=src, dst_ref=dst, send_sem=ssem, recv_sem=rsem, device_id=to, device_id_type=MESH
        )

    barrier = pltpu.get_barrier_semaphore()
    for other in (zp, zm, xp, xm, mate, ynear, yfar):
        pl.semaphore_signal(barrier, inc=1, device_id=other, device_id_type=MESH)

    live_in = pltpu.make_async_copy(live_hbm, live, s_in.at[0])
    w_in = pltpu.make_async_copy(w_hbm, wbuf.at[0, 7], s_in.at[1])
    a_in = [
        pltpu.make_async_copy(a_hbm.at[pl.ds(2 * n, 2)], raw.at[pl.ds(2 * n, 2)], s_in.at[2 + n])
        for n in range(4)
    ]
    live_in.start()
    for n in (0, 2, 1, 3):
        a_in[n].start()
    w_in.start()

    def a_own(side, chunk):
        rows = pl.ds(chunk * 128, 128)
        return rcopy(aown.at[:, rows], abuf.at[side, :, rows], s_a.at[side, chunk], r_a.at[side, chunk],
                     (xp, xm)[side])

    def a_fwd(side, chunk):
        rows = pl.ds(chunk * 128, 128)
        return rcopy(abuf.at[side, :, rows], abuf.at[2, :, rows], s_af.at[chunk], r_a.at[2, chunk],
                     (xp, xm)[side])

    def w_hop(way, step, part):
        k, rows = part // 2, pl.ds((part % 2) * 32, 32)
        src = wbuf.at[0, 7, k, rows] if step == 1 else wbuf.at[way, step - 2, k, rows]
        dst = wbuf.at[1, 7, k, rows] if step == 8 else wbuf.at[way, step - 1, k, rows]
        return rcopy(src, dst, s_w.at[way, step - 1, part], r_w.at[way, step - 1, part], (zm, zp)[way])

    def carried(way, step, part):
        return step < 8 or part // 2 == 1 - way

    live_in.wait()
    block = lax.broadcasted_iota(jnp.int32, (1, 512), 1) // 64
    col = []
    for k in range(2):
        line = jnp.zeros((1, 512), F32)
        for n in range(8):
            line = jnp.where(block == n, live[k, c_index * 8 + n].astype(F32), line)
        col.append(line)

    def mask_chunk(n):
        a_in[n].wait()
        for i in (2 * n, 2 * n + 1):
            both = jnp.transpose(raw[i], (1, 0, 2))
            row = live[i, t_index].astype(F32)
            for k in range(2):
                aown[k, i * 64:(i + 1) * 64] = both[k] * (col[k] * row).astype(BF16)

    mask_chunk(0)
    mask_chunk(2)
    w_in.wait()
    pl.semaphore_wait(barrier, 7)
    for part in range(4):
        for way in range(2):
            w_hop(way, 1, part).start()
    a_own(0, 0).start()
    a_own(1, 2).start()
    mask_chunk(1)
    mask_chunk(3)
    for order in range(1, 4):
        a_own(0, order).start()
        a_own(1, (order + 2) % 4).start()

    def rows_of(n):
        lo, hi = GROUPS[UNITS[n][1]]
        return pl.ds(lo * 64, (hi - lo) * 64)

    def swapped(n):
        stage, group = UNITS[n]
        return (stage + (group > 0)) % 2

    def c_copy(n):
        part = (UNITS[n][0], slice(None), rows_of(n))
        return rcopy(csend.at[part], crecv.at[part], s_c.at[n], r_c.at[n], mate)

    def y1_copy(n, b):
        part = (UNITS[n][0], b, rows_of(n))
        return rcopy(y1send.at[part], y1recv.at[part], s_y1.at[n, b], r_y1.at[n, b],
                     (ynear, yfar)[swapped(n)])

    def y2_copy(n):
        part = (UNITS[n][0], rows_of(n))
        return rcopy(y2send.at[part], y2recv.at[part], s_y2.at[n], r_y2.at[n],
                     (yfar, ynear)[swapped(n)])

    def compute(n):
        stage, group = UNITS[n]
        lo, hi = GROUPS[group]
        size = (hi - lo) * 64
        blocks = abuf.at[stage - 1] if stage else aown

        rows = jnp.concatenate([
            jnp.concatenate([wbuf[core, lo:hi, k].reshape(size, 512) for k in range(2)], axis=1)
            for core in (q, 1 - q)
        ], axis=0)
        for p in range(2):
            cols = slice(p * 256, p * 256 + 256)
            total = dot_nt(rows, jnp.concatenate([blocks[0, cols], blocks[1, cols]], axis=1))
            for b in range(2):
                half = total[:, b * 128:(b + 1) * 128]
                kept[stage, p * 2 + b, rows_of(n)] = half[:size]
                csend[stage, p * 2 + b, rows_of(n)] = half[size:].astype(BF16)
        c_copy(n).start()

    def core_sum(n):
        stage, rows = UNITS[n][0], rows_of(n)
        near, far = (yn3, yn1) if swapped(n) else (yn1, yn3)
        c_copy(n).wait_recv()
        y1send[stage, 1, rows] = (kept[stage, yop, rows] + crecv[stage, yop, rows].astype(F32)).astype(BF16)
        y1_copy(n, 1).start()
        y1send[stage, 0, rows] = (kept[stage, near, rows] + crecv[stage, near, rows].astype(F32)).astype(BF16)
        y1_copy(n, 0).start()
        kept[stage, far, rows] = kept[stage, far, rows] + crecv[stage, far, rows].astype(F32)
        kept[stage, y, rows] = kept[stage, y, rows] + crecv[stage, y, rows].astype(F32)

    def y_sum1(n):
        stage, rows = UNITS[n][0], rows_of(n)
        far = yn1 if swapped(n) else yn3
        y1_copy(n, 1).wait_recv()
        y2send[stage, rows] = (kept[stage, far, rows] + y1recv[stage, 1, rows].astype(F32)).astype(BF16)
        y2_copy(n).start()

    def off(slot):
        return (1 - q) * ((slot + 1) % 8) + q * (15 - slot)

    def p_copy(stage, slot, i):
        return rcopy(psend.at[stage, slot, i], pieces.at[stage, z], s_p.at[stage, slot, i],
                     r_p.at[stage, z], dev(x, y, (z + off(slot)) % NZ, i))

    def half_way(stage, i):
        return rcopy(psend.at[stage, 7, i], relay.at[stage, i], s_p.at[stage, 7, i],
                     r_relay.at[stage, i], dev(x, y, (z + 12) % NZ, q))

    def other_half(stage, i):
        origin = (z + 4) % NZ
        return rcopy(relay.at[stage, i], pieces.at[stage, origin], s_relay.at[stage, i],
                     r_p.at[stage, origin], dev(x, y, (z + 12) % NZ, i))

    def relay_on(stage):
        @pl.when(q != 0)
        def _():
            for i in range(2):
                half_way(stage, i).wait_recv()
                other_half(stage, i).start()

    low = lax.broadcasted_iota(jnp.int32, (32, 128), 1) < 64

    def last_slot(stage, own, away):
        @pl.when(q == 0)
        def _():
            own()

        @pl.when(q != 0)
        def _():
            for i in range(2):
                away(half_way(stage, i) if stage < 2 else p_copy(stage, 7, i))

    def y_sum2(n):
        stage, group = UNITS[n]
        lo, hi = GROUPS[group]
        y1_copy(n, 0).wait_recv()
        y2_copy(n).wait_recv()
        for slot in range(lo, hi):
            rows = slice(slot * 64, (slot + 1) * 64)
            full = (kept[stage, y, rows] + y1recv[stage, 0, rows].astype(F32)
                    + y2recv[stage, rows].astype(F32))
            top, bottom = full[:32], full[32:]
            psend[stage, slot, 0] = jnp.where(low, top, pltpu.roll(bottom, 64, 1)).astype(BF16)
            psend[stage, slot, 1] = jnp.where(low, pltpu.roll(top, 64, 1), bottom).astype(BF16)
        for slot in range(hi - 1, lo - 1, -1):
            if slot < 7:
                p_copy(stage, slot, 0).start()
                p_copy(stage, slot, 1).start()
            else:
                def own():
                    pieces[stage, z] = psend[stage, 7, 0]
                    p_copy(stage, 7, 1).start()

                last_slot(stage, own, lambda copy: copy.start())

    def ring(step):
        for part in range(4):
            for way in range(2):
                w_hop(way, step - 1, part).wait_recv()
                if carried(way, step, part):
                    w_hop(way, step, part).start()

    def forward(first):
        for side in range(2):
            chunk = first + 2 * side
            a_own(side, chunk).wait_recv()
            a_fwd(side, chunk).start()

    ring(2)
    ring(3)
    ring(4)
    ring(5)
    compute(0)
    ring(6)
    forward(0)
    forward(1)
    core_sum(0)
    ring(7)
    y_sum1(0)
    compute(1)
    ring(8)
    core_sum(1)
    y_sum2(0)
    a_own(1, 0).wait_recv()
    a_own(1, 1).wait_recv()
    a_own(0, 2).wait_recv()
    a_own(0, 3).wait_recv()
    compute(7)
    for part in range(2):
        w_hop(0, 8, part + 2).wait_recv()
        w_hop(1, 8, part).wait_recv()
    compute(4)
    compute(3)
    y_sum1(1)
    core_sum(7)
    compute(2)
    core_sum(4)
    compute(5)
    compute(8)
    core_sum(2)
    y_sum1(7)
    core_sum(5)
    compute(6)
    core_sum(8)
    y_sum2(1)
    y_sum1(4)
    y_sum1(2)
    core_sum(6)
    y_sum2(7)
    for chunk in range(4):
        a_fwd(chunk // 2, chunk).wait_recv()
    y_sum1(5)
    compute(11)
    core_sum(3)
    y_sum1(8)
    y_sum2(2)
    y_sum2(4)
    core_sum(11)
    y_sum2(5)
    y_sum1(6)
    compute(9)
    y_sum1(3)
    y_sum2(8)
    compute(10)
    y_sum1(11)
    core_sum(9)
    core_sum(10)
    y_sum2(6)
    y_sum2(3)
    y_sum1(10)
    y_sum1(9)
    relay_on(1)
    y_sum2(11)
    relay_on(0)
    y_sum2(10)
    y_sum2(9)

    for stage in range(4):
        xs = (x + (0, 3, 1, 2)[stage]) % 4

        def arrive(n, carry):
            @pl.when((n != z) | (q != 0))
            def _():
                rcopy(psend.at[0, 0, 0], pieces.at[stage, n], s_p.at[0, 0, 0], r_p.at[stage, n],
                      mate).wait_recv()

            return carry

        lax.fori_loop(0, NZ, arrive, 0)
        for m in range(NZ // 2):
            even, odd = pieces[stage, 2 * m].astype(F32), pieces[stage, 2 * m + 1].astype(F32)
            cols = pl.ds(pl.multiple_of(xs * 1024 + m * 128, 128), 128)
            out_ref[0:32, cols] = jnp.where(low, even, pltpu.roll(odd, 64, 1)).astype(BF16)
            out_ref[32:64, cols] = jnp.where(low, pltpu.roll(even, 64, 1), odd).astype(BF16)

    for way in range(2):
        for n in range(1, 9):
            for part in range(4):
                if carried(way, n, part):
                    w_hop(way, n, part).wait_send()
        for chunk in range(4):
            a_own(way, chunk).wait_send()
    for chunk in range(4):
        a_fwd(chunk // 2, chunk).wait_send()
    for n in range(len(UNITS)):
        c_copy(n).wait_send()
        y1_copy(n, 0).wait_send()
        y1_copy(n, 1).wait_send()
        y2_copy(n).wait_send()
    for stage in range(4):
        for slot in range(7):
            p_copy(stage, slot, 0).wait_send()
            p_copy(stage, slot, 1).wait_send()
        last_slot(stage, lambda: p_copy(stage, 7, 1).wait_send(), lambda copy: copy.wait_send())

    @pl.when(q != 0)
    def _():
        for stage in range(2):
            for i in range(2):
                other_half(stage, i).wait_send()


def fused(amplitudes, tiles, pair_live):
    dma = pltpu.SemaphoreType.DMA
    return pl.pallas_call(
        kernel,
        out_shape=jax.ShapeDtypeStruct((64, 4096), BF16),
        in_specs=[pl.BlockSpec(memory_space=pl.ANY)] * 3,
        out_specs=pl.BlockSpec(memory_space=pltpu.VMEM),
        scratch_shapes=[
            pltpu.VMEM((8, 64, 2, 512), BF16),
            pltpu.SMEM((8, 64), jnp.int32),
            pltpu.VMEM((2, 512, 512), BF16),
            pltpu.VMEM((3, 2, 512, 512), BF16),
            pltpu.VMEM((2, 8, 2, 64, 512), BF16),
            pltpu.VMEM((4, 4, 512, 128), F32),
            pltpu.VMEM((4, 4, 512, 128), BF16),
            pltpu.VMEM((4, 4, 512, 128), BF16),
            pltpu.VMEM((4, 2, 512, 128), BF16),
            pltpu.VMEM((4, 2, 512, 128), BF16),
            pltpu.VMEM((4, 512, 128), BF16),
            pltpu.VMEM((4, 512, 128), BF16),
            pltpu.VMEM((4, 8, 2, 32, 128), BF16),
            pltpu.VMEM((4, NZ, 32, 128), BF16),
            pltpu.VMEM((2, 2, 32, 128), BF16),
            dma((6,)), dma((2, 4)), dma((4,)), dma((3, 4)),
            dma((2, 8, 4)), dma((2, 8, 4)),
            dma((12,)), dma((12,)), dma((12, 2)), dma((12, 2)), dma((12,)), dma((12,)),
            dma((4, 8, 2)), dma((4, NZ)), dma((2, 2)), dma((2, 2)),
        ],
        compiler_params=pltpu.CompilerParams(
            collective_id=0, has_side_effects=True, vmem_limit_bytes=40 * 1024 * 1024
        ),
        name="cycle_fused",
    )(amplitudes, tiles, pair_live)


def per_device(amplitudes, cycle_integrals, pair_live):
    tiles = cycle_integrals[:, :, 0, :].transpose(0, 2, 1)
    operands = [
        pltpu.with_memory_space_constraint(operand, pltpu.HBM)
        for operand in (amplitudes, tiles, pair_live)
    ]
    return fused(*operands).reshape(1, 64, 1, 4096)


def solution(mesh):
    return jax.shard_map(
        per_device,
        mesh=mesh,
        in_specs=(P(None, "tr", None, "ct"), P(None, "ct", None, "tr"), P()),
        out_specs=P("ct", "tr", None, None),
        check_vma=False,
    )
```

```python
import functools

import jax
import jax.numpy as jnp
from jax import lax
from jax.experimental import pallas as pl
from jax.experimental.pallas import tpu as pltpu
from jax.sharding import PartitionSpec as P

MESH = pl.DeviceIdType.MESH
F32 = jnp.float32
BF16 = jnp.bfloat16
NZ = 16
GROUPS = ((0, 4), (4, 6), (6, 8))
UNITS = [(stage, group) for stage in range(4) for group in range(3)]


def dot_nt(lhs, rhs):
    return lax.dot_general(lhs, rhs, (((1,), (1,)), ((), ())), preferred_element_type=F32)


def kernel(
    a_hbm, w_hbm, live_hbm, out_ref,
    raw, live, aown, abuf, wbuf, kept, csend, crecv, y1send, y1recv, y2send, y2recv, psend, pieces, relay,
    s_in, s_a, s_af, r_a, s_w, r_w, s_c, r_c, s_y1, r_y1, s_y2, r_y2, s_p, r_p, s_relay, r_relay,
):
    t_index = lax.axis_index("tr")
    c_index = lax.axis_index("ct")
    x, z = t_index // NZ, t_index % NZ
    y, q = c_index // 2, c_index % 2
    yn1 = y + 1 - 2 * (y % 2)
    yn3 = 3 - y
    yop = (y + 2) % 4

    def dev(xx, yy, zz, qq):
        return (xx * NZ + zz, yy * 2 + qq)

    xp, xm = dev((x + 1) % 4, y, z, q), dev((x + 3) % 4, y, z, q)
    zp, zm = dev(x, y, (z + 1) % NZ, q), dev(x, y, (z + NZ - 1) % NZ, q)
    mate = dev(x, y, z, 1 - q)
    ynear, yfar = dev(x, yn1, z, q), dev(x, yn3, z, q)

    def rcopy(src, dst, ssem, rsem, to):
        return pltpu.make_async_remote_copy(
            src_ref=src, dst_ref=dst, send_sem=ssem, recv_sem=rsem, device_id=to, device_id_type=MESH
        )

    barrier = pltpu.get_barrier_semaphore()
    for other in (zp, zm, xp, xm, mate, ynear, yfar):
        pl.semaphore_signal(barrier, inc=1, device_id=other, device_id_type=MESH)

    live_in = pltpu.make_async_copy(live_hbm, live, s_in.at[0])
    w_in = pltpu.make_async_copy(w_hbm, wbuf.at[0, 7], s_in.at[1])
    a_in = [
        pltpu.make_async_copy(a_hbm.at[pl.ds(2 * n, 2)], raw.at[pl.ds(2 * n, 2)], s_in.at[2 + n])
        for n in range(4)
    ]
    live_in.start()
    for n in (0, 2, 1, 3):
        a_in[n].start()
    w_in.start()

    def a_own(side, chunk):
        rows = pl.ds(chunk * 128, 128)
        return rcopy(aown.at[:, rows], abuf.at[side, :, rows], s_a.at[side, chunk], r_a.at[side, chunk],
                     (xp, xm)[side])

    def a_fwd(side, chunk):
        rows = pl.ds(chunk * 128, 128)
        return rcopy(abuf.at[side, :, rows], abuf.at[2, :, rows], s_af.at[chunk], r_a.at[2, chunk],
                     (xp, xm)[side])

    def w_hop(way, step, part):
        k, rows = part // 2, pl.ds((part % 2) * 32, 32)
        src = wbuf.at[0, 7, k, rows] if step == 1 else wbuf.at[way, step - 2, k, rows]
        dst = wbuf.at[1, 7, k, rows] if step == 8 else wbuf.at[way, step - 1, k, rows]
        return rcopy(src, dst, s_w.at[way, step - 1, part], r_w.at[way, step - 1, part], (zm, zp)[way])

    def carried(way, step, part):
        return step < 8 or part // 2 == 1 - way

    live_in.wait()
    block = lax.broadcasted_iota(jnp.int32, (1, 512), 1) // 64
    col = []
    for k in range(2):
        line = jnp.zeros((1, 512), F32)
        for n in range(8):
            line = jnp.where(block == n, live[k, c_index * 8 + n].astype(F32), line)
        col.append(line)

    def mask_chunk(n):
        a_in[n].wait()
        for i in (2 * n, 2 * n + 1):
            both = jnp.transpose(raw[i], (1, 0, 2))
            row = live[i, t_index].astype(F32)
            for k in range(2):
                aown[k, i * 64:(i + 1) * 64] = both[k] * (col[k] * row).astype(BF16)

    mask_chunk(0)
    mask_chunk(2)
    w_in.wait()
    pl.semaphore_wait(barrier, 7)
    for part in range(4):
        for way in range(2):
            w_hop(way, 1, part).start()
    a_own(0, 0).start()
    a_own(1, 2).start()
    mask_chunk(1)
    mask_chunk(3)
    for order in range(1, 4):
        a_own(0, order).start()
        a_own(1, (order + 2) % 4).start()

    def rows_of(n):
        lo, hi = GROUPS[UNITS[n][1]]
        return pl.ds(lo * 64, (hi - lo) * 64)

    def swapped(n):
        stage, group = UNITS[n]
        return (stage + (group > 0)) % 2

    def c_copy(n):
        part = (UNITS[n][0], slice(None), rows_of(n))
        return rcopy(csend.at[part], crecv.at[part], s_c.at[n], r_c.at[n], mate)

    def y1_copy(n, b):
        part = (UNITS[n][0], b, rows_of(n))
        return rcopy(y1send.at[part], y1recv.at[part], s_y1.at[n, b], r_y1.at[n, b],
                     (ynear, yfar)[swapped(n)])

    def y2_copy(n):
        part = (UNITS[n][0], rows_of(n))
        return rcopy(y2send.at[part], y2recv.at[part], s_y2.at[n], r_y2.at[n],
                     (yfar, ynear)[swapped(n)])

    def compute(n):
        stage, group = UNITS[n]
        lo, hi = GROUPS[group]
        size = (hi - lo) * 64
        blocks = abuf.at[stage - 1] if stage else aown

        rows = jnp.concatenate([
            jnp.concatenate([wbuf[core, lo:hi, k].reshape(size, 512) for k in range(2)], axis=1)
            for core in (q, 1 - q)
        ], axis=0)
        for p in range(2):
            cols = slice(p * 256, p * 256 + 256)
            total = dot_nt(rows, jnp.concatenate([blocks[0, cols], blocks[1, cols]], axis=1))
            for b in range(2):
                half = total[:, b * 128:(b + 1) * 128]
                kept[stage, p * 2 + b, rows_of(n)] = half[:size]
                csend[stage, p * 2 + b, rows_of(n)] = half[size:].astype(BF16)
        c_copy(n).start()

    def core_sum(n):
        stage, rows = UNITS[n][0], rows_of(n)
        near, far = (yn3, yn1) if swapped(n) else (yn1, yn3)
        c_copy(n).wait_recv()
        y1send[stage, 1, rows] = (kept[stage, yop, rows] + crecv[stage, yop, rows].astype(F32)).astype(BF16)
        y1_copy(n, 1).start()
        y1send[stage, 0, rows] = (kept[stage, near, rows] + crecv[stage, near, rows].astype(F32)).astype(BF16)
        y1_copy(n, 0).start()
        kept[stage, far, rows] = kept[stage, far, rows] + crecv[stage, far, rows].astype(F32)
        kept[stage, y, rows] = kept[stage, y, rows] + crecv[stage, y, rows].astype(F32)

    def y_sum1(n):
        stage, rows = UNITS[n][0], rows_of(n)
        far = yn1 if swapped(n) else yn3
        y1_copy(n, 1).wait_recv()
        y2send[stage, rows] = (kept[stage, far, rows] + y1recv[stage, 1, rows].astype(F32)).astype(BF16)
        y2_copy(n).start()

    def off(slot):
        return (1 - q) * ((slot + 1) % 8) + q * (15 - slot)

    def p_copy(stage, slot, i):
        return rcopy(psend.at[stage, slot, i], pieces.at[stage, z], s_p.at[stage, slot, i],
                     r_p.at[stage, z], dev(x, y, (z + off(slot)) % NZ, i))

    def half_way(stage, i):
        return rcopy(psend.at[stage, 7, i], relay.at[stage, i], s_p.at[stage, 7, i],
                     r_relay.at[stage, i], dev(x, y, (z + 12) % NZ, q))

    def other_half(stage, i):
        origin = (z + 4) % NZ
        return rcopy(relay.at[stage, i], pieces.at[stage, origin], s_relay.at[stage, i],
                     r_p.at[stage, origin], dev(x, y, (z + 12) % NZ, i))

    def relay_on(stage):
        @pl.when(q != 0)
        def _():
            for i in range(2):
                half_way(stage, i).wait_recv()
                other_half(stage, i).start()

    low = lax.broadcasted_iota(jnp.int32, (32, 128), 1) < 64

    def last_slot(stage, own, away):
        @pl.when(q == 0)
        def _():
            own()

        @pl.when(q != 0)
        def _():
            for i in range(2):
                away(half_way(stage, i) if stage < 2 else p_copy(stage, 7, i))

    def y_sum2(n):
        stage, group = UNITS[n]
        lo, hi = GROUPS[group]
        y1_copy(n, 0).wait_recv()
        y2_copy(n).wait_recv()
        for slot in range(lo, hi):
            rows = slice(slot * 64, (slot + 1) * 64)
            full = (kept[stage, y, rows] + y1recv[stage, 0, rows].astype(F32)
                    + y2recv[stage, rows].astype(F32))
            top, bottom = full[:32], full[32:]
            psend[stage, slot, 0] = jnp.where(low, top, pltpu.roll(bottom, 64, 1)).astype(BF16)
            psend[stage, slot, 1] = jnp.where(low, pltpu.roll(top, 64, 1), bottom).astype(BF16)
        for slot in range(hi - 1, lo - 1, -1):
            if slot < 7:
                p_copy(stage, slot, 0).start()
                p_copy(stage, slot, 1).start()
            else:
                def own():
                    pieces[stage, z] = psend[stage, 7, 0]
                    p_copy(stage, 7, 1).start()

                last_slot(stage, own, lambda copy: copy.start())

    def ring(step):
        for part in range(4):
            for way in range(2):
                w_hop(way, step - 1, part).wait_recv()
                if carried(way, step, part):
                    w_hop(way, step, part).start()

    def forward(first):
        for side in range(2):
            chunk = first + 2 * side
            a_own(side, chunk).wait_recv()
            a_fwd(side, chunk).start()

    ring(2)
    ring(3)
    ring(4)
    ring(5)
    compute(0)
    ring(6)
    forward(0)
    forward(1)
    core_sum(0)
    ring(7)
    y_sum1(0)
    compute(1)
    ring(8)
    core_sum(1)
    y_sum2(0)
    a_own(1, 0).wait_recv()
    a_own(1, 1).wait_recv()
    a_own(0, 2).wait_recv()
    a_own(0, 3).wait_recv()
    compute(7)
    for part in range(2):
        w_hop(0, 8, part + 2).wait_recv()
        w_hop(1, 8, part).wait_recv()
    compute(4)
    compute(3)
    y_sum1(1)
    core_sum(7)
    compute(2)
    core_sum(4)
    compute(5)
    compute(8)
    core_sum(2)
    y_sum1(7)
    core_sum(5)
    compute(6)
    core_sum(8)
    y_sum2(1)
    y_sum1(4)
    y_sum1(2)
    core_sum(6)
    y_sum2(7)
    for chunk in range(4):
        a_fwd(chunk // 2, chunk).wait_recv()
    y_sum1(5)
    compute(11)
    core_sum(3)
    y_sum1(8)
    y_sum2(2)
    y_sum2(4)
    core_sum(11)
    y_sum2(5)
    y_sum1(6)
    compute(9)
    y_sum1(3)
    y_sum2(8)
    compute(10)
    y_sum1(11)
    core_sum(9)
    core_sum(10)
    y_sum2(6)
    y_sum2(3)
    y_sum1(10)
    y_sum1(9)
    relay_on(1)
    y_sum2(11)
    relay_on(0)
    y_sum2(10)
    y_sum2(9)

    for way in range(2):
        for n in range(1, 9):
            for part in range(4):
                if carried(way, n, part):
                    w_hop(way, n, part).wait_send()
        for chunk in range(4):
            a_own(way, chunk).wait_send()
    for chunk in range(4):
        a_fwd(chunk // 2, chunk).wait_send()
    for n in range(len(UNITS)):
        c_copy(n).wait_send()
        y1_copy(n, 0).wait_send()
        y1_copy(n, 1).wait_send()
        y2_copy(n).wait_send()

    def unpack(stage):
        xs = (x + (0, 3, 1, 2)[stage]) % 4

        def arrive(n, carry):
            @pl.when((n != z) | (q != 0))
            def _():
                rcopy(psend.at[0, 0, 0], pieces.at[stage, n], s_p.at[0, 0, 0], r_p.at[stage, n],
                      mate).wait_recv()

            return carry

        lax.fori_loop(0, NZ, arrive, 0)
        for m in range(NZ // 2):
            even, odd = pieces[stage, 2 * m].astype(F32), pieces[stage, 2 * m + 1].astype(F32)
            cols = pl.ds(pl.multiple_of(xs * 1024 + m * 128, 128), 128)
            out_ref[0:32, cols] = jnp.where(low, even, pltpu.roll(odd, 64, 1)).astype(BF16)
            out_ref[32:64, cols] = jnp.where(low, pltpu.roll(even, 64, 1), odd).astype(BF16)

    for stage in range(3):
        unpack(stage)

    for stage in range(4):
        for slot in range(7):
            p_copy(stage, slot, 0).wait_send()
            p_copy(stage, slot, 1).wait_send()
        last_slot(stage, lambda: p_copy(stage, 7, 1).wait_send(), lambda copy: copy.wait_send())

    @pl.when(q != 0)
    def _():
        for stage in range(2):
            for i in range(2):
                other_half(stage, i).wait_send()

    unpack(3)


def fused(amplitudes, tiles, pair_live):
    dma = pltpu.SemaphoreType.DMA
    return pl.pallas_call(
        kernel,
        out_shape=jax.ShapeDtypeStruct((64, 4096), BF16),
        in_specs=[pl.BlockSpec(memory_space=pl.ANY)] * 3,
        out_specs=pl.BlockSpec(memory_space=pltpu.VMEM),
        scratch_shapes=[
            pltpu.VMEM((8, 64, 2, 512), BF16),
            pltpu.SMEM((8, 64), jnp.int32),
            pltpu.VMEM((2, 512, 512), BF16),
            pltpu.VMEM((3, 2, 512, 512), BF16),
            pltpu.VMEM((2, 8, 2, 64, 512), BF16),
            pltpu.VMEM((4, 4, 512, 128), F32),
            pltpu.VMEM((4, 4, 512, 128), BF16),
            pltpu.VMEM((4, 4, 512, 128), BF16),
            pltpu.VMEM((4, 2, 512, 128), BF16),
            pltpu.VMEM((4, 2, 512, 128), BF16),
            pltpu.VMEM((4, 512, 128), BF16),
            pltpu.VMEM((4, 512, 128), BF16),
            pltpu.VMEM((4, 8, 2, 32, 128), BF16),
            pltpu.VMEM((4, NZ, 32, 128), BF16),
            pltpu.VMEM((2, 2, 32, 128), BF16),
            dma((6,)), dma((2, 4)), dma((4,)), dma((3, 4)),
            dma((2, 8, 4)), dma((2, 8, 4)),
            dma((12,)), dma((12,)), dma((12, 2)), dma((12, 2)), dma((12,)), dma((12,)),
            dma((4, 8, 2)), dma((4, NZ)), dma((2, 2)), dma((2, 2)),
        ],
        compiler_params=pltpu.CompilerParams(
            collective_id=0, has_side_effects=True, vmem_limit_bytes=40 * 1024 * 1024
        ),
        name="cycle_fused",
    )(amplitudes, tiles, pair_live)


def per_device(amplitudes, cycle_integrals, pair_live):
    tiles = cycle_integrals[:, :, 0, :].transpose(0, 2, 1)
    operands = [
        pltpu.with_memory_space_constraint(operand, pltpu.HBM)
        for operand in (amplitudes, tiles, pair_live)
    ]
    return fused(*operands).reshape(1, 64, 1, 4096)


def solution(mesh):
    return jax.shard_map(
        per_device,
        mesh=mesh,
        in_specs=(P(None, "tr", None, "ct"), P(None, "ct", None, "tr"), P()),
        out_specs=P("ct", "tr", None, None),
        check_vma=False,
    )
```

```python
import functools

import jax
import jax.numpy as jnp
from jax import lax
from jax.experimental import pallas as pl
from jax.experimental.pallas import tpu as pltpu
from jax.sharding import PartitionSpec as P

MESH = pl.DeviceIdType.MESH
F32 = jnp.float32
BF16 = jnp.bfloat16
NZ = 16
GROUPS = ((0, 4), (4, 6), (6, 8))
UNITS = [(stage, group) for stage in range(4) for group in range(3)]


def dot_nt(lhs, rhs):
    return lax.dot_general(lhs, rhs, (((1,), (1,)), ((), ())), preferred_element_type=F32)


def kernel(
    a_hbm, w_hbm, live_hbm, out_ref,
    raw, live, aown, abuf, wbuf, kept, csend, crecv, y1send, y1recv, y2send, y2recv, psend, pieces, relay,
    s_in, s_a, s_af, r_a, s_w, r_w, s_c, r_c, s_y1, r_y1, s_y2, r_y2, s_p, r_p, s_relay, r_relay,
):
    t_index = lax.axis_index("tr")
    c_index = lax.axis_index("ct")
    x, z = t_index // NZ, t_index % NZ
    y, q = c_index // 2, c_index % 2
    yn1 = y + 1 - 2 * (y % 2)
    yn3 = 3 - y
    yop = (y + 2) % 4

    def dev(xx, yy, zz, qq):
        return (xx * NZ + zz, yy * 2 + qq)

    xp, xm = dev((x + 1) % 4, y, z, q), dev((x + 3) % 4, y, z, q)
    zp, zm = dev(x, y, (z + 1) % NZ, q), dev(x, y, (z + NZ - 1) % NZ, q)
    mate = dev(x, y, z, 1 - q)
    ynear, yfar = dev(x, yn1, z, q), dev(x, yn3, z, q)

    def rcopy(src, dst, ssem, rsem, to):
        return pltpu.make_async_remote_copy(
            src_ref=src, dst_ref=dst, send_sem=ssem, recv_sem=rsem, device_id=to, device_id_type=MESH
        )

    barrier = pltpu.get_barrier_semaphore()
    for other in (zp, zm, xp, xm, mate, ynear, yfar):
        pl.semaphore_signal(barrier, inc=1, device_id=other, device_id_type=MESH)

    live_in = pltpu.make_async_copy(live_hbm, live, s_in.at[0])
    w_in = pltpu.make_async_copy(w_hbm, wbuf.at[0, 7], s_in.at[1])
    a_in = [
        pltpu.make_async_copy(a_hbm.at[pl.ds(2 * n, 2)], raw.at[pl.ds(2 * n, 2)], s_in.at[2 + n])
        for n in range(4)
    ]
    live_in.start()
    for n in (0, 2, 1, 3):
        a_in[n].start()
    w_in.start()

    def a_own(side, chunk):
        rows = pl.ds(chunk * 128, 128)
        return rcopy(aown.at[:, rows], abuf.at[side, :, rows], s_a.at[side, chunk], r_a.at[side, chunk],
                     (xp, xm)[side])

    def a_fwd(side, chunk):
        rows = pl.ds(chunk * 128, 128)
        return rcopy(abuf.at[side, :, rows], abuf.at[2, :, rows], s_af.at[chunk], r_a.at[2, chunk],
                     (xp, xm)[side])

    def w_hop(way, step, part):
        k, rows = part // 2, pl.ds((part % 2) * 32, 32)
        src = wbuf.at[0, 7, k, rows] if step == 1 else wbuf.at[way, step - 2, k, rows]
        dst = wbuf.at[1, 7, k, rows] if step == 8 else wbuf.at[way, step - 1, k, rows]
        return rcopy(src, dst, s_w.at[way, step - 1, part], r_w.at[way, step - 1, part], (zm, zp)[way])

    def carried(way, step, part):
        return step < 8 or part // 2 == 1 - way

    live_in.wait()
    block = lax.broadcasted_iota(jnp.int32, (1, 512), 1) // 64
    col = []
    for k in range(2):
        line = jnp.zeros((1, 512), F32)
        for n in range(8):
            line = jnp.where(block == n, live[k, c_index * 8 + n].astype(F32), line)
        col.append(line)

    def mask_chunk(n):
        a_in[n].wait()
        for i in (2 * n, 2 * n + 1):
            both = jnp.transpose(raw[i], (1, 0, 2))
            row = live[i, t_index].astype(F32)
            for k in range(2):
                aown[k, i * 64:(i + 1) * 64] = both[k] * (col[k] * row).astype(BF16)

    for chunk in (0, 2, 1, 3):
        mask_chunk(chunk)
    w_in.wait()
    pl.semaphore_wait(barrier, 7)
    for part in range(4):
        for way in range(2):
            w_hop(way, 1, part).start()
    a_own(0, 0).start()
    a_own(1, 2).start()
    for order in range(1, 4):
        a_own(0, order).start()
        a_own(1, (order + 2) % 4).start()

    def rows_of(n):
        lo, hi = GROUPS[UNITS[n][1]]
        return pl.ds(lo * 64, (hi - lo) * 64)

    def swapped(n):
        stage, group = UNITS[n]
        return (stage + (group > 0)) % 2

    def c_copy(n):
        part = (UNITS[n][0], slice(None), rows_of(n))
        return rcopy(csend.at[part], crecv.at[part], s_c.at[n], r_c.at[n], mate)

    def y1_copy(n, b):
        part = (UNITS[n][0], b, rows_of(n))
        return rcopy(y1send.at[part], y1recv.at[part], s_y1.at[n, b], r_y1.at[n, b],
                     (ynear, yfar)[swapped(n)])

    def y2_copy(n):
        part = (UNITS[n][0], rows_of(n))
        return rcopy(y2send.at[part], y2recv.at[part], s_y2.at[n], r_y2.at[n],
                     (yfar, ynear)[swapped(n)])

    def compute(n):
        stage, group = UNITS[n]
        lo, hi = GROUPS[group]
        size = (hi - lo) * 64
        blocks = abuf.at[stage - 1] if stage else aown

        rows = jnp.concatenate([
            jnp.concatenate([wbuf[core, lo:hi, k].reshape(size, 512) for k in range(2)], axis=1)
            for core in (q, 1 - q)
        ], axis=0)
        for p in range(2):
            cols = slice(p * 256, p * 256 + 256)
            total = dot_nt(rows, jnp.concatenate([blocks[0, cols], blocks[1, cols]], axis=1))
            for b in range(2):
                half = total[:, b * 128:(b + 1) * 128]
                kept[stage, p * 2 + b, rows_of(n)] = half[:size]
                csend[stage, p * 2 + b, rows_of(n)] = half[size:].astype(BF16)
        c_copy(n).start()

    def core_sum(n):
        stage, rows = UNITS[n][0], rows_of(n)
        near, far = (yn3, yn1) if swapped(n) else (yn1, yn3)
        c_copy(n).wait_recv()
        y1send[stage, 1, rows] = (kept[stage, yop, rows] + crecv[stage, yop, rows].astype(F32)).astype(BF16)
        y1_copy(n, 1).start()
        y1send[stage, 0, rows] = (kept[stage, near, rows] + crecv[stage, near, rows].astype(F32)).astype(BF16)
        y1_copy(n, 0).start()
        kept[stage, far, rows] = kept[stage, far, rows] + crecv[stage, far, rows].astype(F32)
        kept[stage, y, rows] = kept[stage, y, rows] + crecv[stage, y, rows].astype(F32)

    def y_sum1(n):
        stage, rows = UNITS[n][0], rows_of(n)
        far = yn1 if swapped(n) else yn3
        y1_copy(n, 1).wait_recv()
        y2send[stage, rows] = (kept[stage, far, rows] + y1recv[stage, 1, rows].astype(F32)).astype(BF16)
        y2_copy(n).start()

    def off(slot):
        return (1 - q) * ((slot + 1) % 8) + q * (15 - slot)

    def p_copy(stage, slot, i):
        return rcopy(psend.at[stage, slot, i], pieces.at[stage, z], s_p.at[stage, slot, i],
                     r_p.at[stage, z], dev(x, y, (z + off(slot)) % NZ, i))

    def half_way(stage, i):
        return rcopy(psend.at[stage, 7, i], relay.at[stage, i], s_p.at[stage, 7, i],
                     r_relay.at[stage, i], dev(x, y, (z + 12) % NZ, q))

    def other_half(stage, i):
        origin = (z + 4) % NZ
        return rcopy(relay.at[stage, i], pieces.at[stage, origin], s_relay.at[stage, i],
                     r_p.at[stage, origin], dev(x, y, (z + 12) % NZ, i))

    def relay_on(stage):
        @pl.when(q != 0)
        def _():
            for i in range(2):
                half_way(stage, i).wait_recv()
                other_half(stage, i).start()

    low = lax.broadcasted_iota(jnp.int32, (32, 128), 1) < 64

    def last_slot(stage, own, away):
        @pl.when(q == 0)
        def _():
            own()

        @pl.when(q != 0)
        def _():
            for i in range(2):
                away(half_way(stage, i) if stage < 2 else p_copy(stage, 7, i))

    def y_sum2(n):
        stage, group = UNITS[n]
        lo, hi = GROUPS[group]
        y1_copy(n, 0).wait_recv()
        y2_copy(n).wait_recv()
        for slot in range(lo, hi):
            rows = slice(slot * 64, (slot + 1) * 64)
            full = (kept[stage, y, rows] + y1recv[stage, 0, rows].astype(F32)
                    + y2recv[stage, rows].astype(F32))
            top, bottom = full[:32], full[32:]
            psend[stage, slot, 0] = jnp.where(low, top, pltpu.roll(bottom, 64, 1)).astype(BF16)
            psend[stage, slot, 1] = jnp.where(low, pltpu.roll(top, 64, 1), bottom).astype(BF16)
        for slot in range(hi - 1, lo - 1, -1):
            if slot < 7:
                p_copy(stage, slot, 0).start()
                p_copy(stage, slot, 1).start()
            else:
                def own():
                    pieces[stage, z] = psend[stage, 7, 0]
                    p_copy(stage, 7, 1).start()

                last_slot(stage, own, lambda copy: copy.start())

    def ring(step):
        for part in range(4):
            for way in range(2):
                w_hop(way, step - 1, part).wait_recv()
                if carried(way, step, part):
                    w_hop(way, step, part).start()

    def forward(first):
        for side in range(2):
            chunk = first + 2 * side
            a_own(side, chunk).wait_recv()
            a_fwd(side, chunk).start()

    ring(2)
    ring(3)
    ring(4)
    ring(5)
    compute(0)
    ring(6)
    forward(0)
    forward(1)
    core_sum(0)
    ring(7)
    y_sum1(0)
    compute(1)
    ring(8)
    core_sum(1)
    y_sum2(0)
    a_own(1, 0).wait_recv()
    a_own(1, 1).wait_recv()
    a_own(0, 2).wait_recv()
    a_own(0, 3).wait_recv()
    compute(7)
    for part in range(2):
        w_hop(0, 8, part + 2).wait_recv()
        w_hop(1, 8, part).wait_recv()
    compute(4)
    compute(3)
    y_sum1(1)
    core_sum(7)
    compute(2)
    core_sum(4)
    compute(5)
    compute(8)
    core_sum(2)
    y_sum1(7)
    core_sum(5)
    compute(6)
    core_sum(8)
    y_sum2(1)
    y_sum1(4)
    y_sum1(2)
    core_sum(6)
    y_sum2(7)
    for chunk in range(4):
        a_fwd(chunk // 2, chunk).wait_recv()
    y_sum1(5)
    compute(11)
    core_sum(3)
    y_sum1(8)
    y_sum2(2)
    y_sum2(4)
    core_sum(11)
    y_sum2(5)
    y_sum1(6)
    compute(9)
    y_sum1(3)
    y_sum2(8)
    compute(10)
    y_sum1(11)
    core_sum(9)
    core_sum(10)
    y_sum2(6)
    y_sum2(3)
    y_sum1(10)
    y_sum1(9)
    relay_on(1)
    y_sum2(11)
    relay_on(0)
    y_sum2(10)
    y_sum2(9)

    for way in range(2):
        for n in range(1, 9):
            for part in range(4):
                if carried(way, n, part):
                    w_hop(way, n, part).wait_send()
        for chunk in range(4):
            a_own(way, chunk).wait_send()
    for chunk in range(4):
        a_fwd(chunk // 2, chunk).wait_send()
    for n in range(len(UNITS)):
        c_copy(n).wait_send()
        y1_copy(n, 0).wait_send()
        y1_copy(n, 1).wait_send()
        y2_copy(n).wait_send()

    def unpack(stage):
        xs = (x + (0, 3, 1, 2)[stage]) % 4

        def arrive(n, carry):
            @pl.when((n != z) | (q != 0))
            def _():
                rcopy(psend.at[0, 0, 0], pieces.at[stage, n], s_p.at[0, 0, 0], r_p.at[stage, n],
                      mate).wait_recv()

            return carry

        lax.fori_loop(0, NZ, arrive, 0)
        for m in range(NZ // 2):
            even, odd = pieces[stage, 2 * m].astype(F32), pieces[stage, 2 * m + 1].astype(F32)
            cols = pl.ds(pl.multiple_of(xs * 1024 + m * 128, 128), 128)
            out_ref[0:32, cols] = jnp.where(low, even, pltpu.roll(odd, 64, 1)).astype(BF16)
            out_ref[32:64, cols] = jnp.where(low, pltpu.roll(even, 64, 1), odd).astype(BF16)

    for stage in range(3):
        unpack(stage)

    for stage in range(4):
        for slot in range(7):
            p_copy(stage, slot, 0).wait_send()
            p_copy(stage, slot, 1).wait_send()
        last_slot(stage, lambda: p_copy(stage, 7, 1).wait_send(), lambda copy: copy.wait_send())

    @pl.when(q != 0)
    def _():
        for stage in range(2):
            for i in range(2):
                other_half(stage, i).wait_send()

    unpack(3)


def fused(amplitudes, tiles, pair_live):
    dma = pltpu.SemaphoreType.DMA
    return pl.pallas_call(
        kernel,
        out_shape=jax.ShapeDtypeStruct((64, 4096), BF16),
        in_specs=[pl.BlockSpec(memory_space=pl.ANY)] * 3,
        out_specs=pl.BlockSpec(memory_space=pltpu.VMEM),
        scratch_shapes=[
            pltpu.VMEM((8, 64, 2, 512), BF16),
            pltpu.SMEM((8, 64), jnp.int32),
            pltpu.VMEM((2, 512, 512), BF16),
            pltpu.VMEM((3, 2, 512, 512), BF16),
            pltpu.VMEM((2, 8, 2, 64, 512), BF16),
            pltpu.VMEM((4, 4, 512, 128), F32),
            pltpu.VMEM((4, 4, 512, 128), BF16),
            pltpu.VMEM((4, 4, 512, 128), BF16),
            pltpu.VMEM((4, 2, 512, 128), BF16),
            pltpu.VMEM((4, 2, 512, 128), BF16),
            pltpu.VMEM((4, 512, 128), BF16),
            pltpu.VMEM((4, 512, 128), BF16),
            pltpu.VMEM((4, 8, 2, 32, 128), BF16),
            pltpu.VMEM((4, NZ, 32, 128), BF16),
            pltpu.VMEM((2, 2, 32, 128), BF16),
            dma((6,)), dma((2, 4)), dma((4,)), dma((3, 4)),
            dma((2, 8, 4)), dma((2, 8, 4)),
            dma((12,)), dma((12,)), dma((12, 2)), dma((12, 2)), dma((12,)), dma((12,)),
            dma((4, 8, 2)), dma((4, NZ)), dma((2, 2)), dma((2, 2)),
        ],
        compiler_params=pltpu.CompilerParams(
            collective_id=0, has_side_effects=True, vmem_limit_bytes=40 * 1024 * 1024
        ),
        name="cycle_fused",
    )(amplitudes, tiles, pair_live)


def per_device(amplitudes, cycle_integrals, pair_live):
    tiles = cycle_integrals[:, :, 0, :].transpose(0, 2, 1)
    operands = [
        pltpu.with_memory_space_constraint(operand, pltpu.HBM)
        for operand in (amplitudes, tiles, pair_live)
    ]
    return fused(*operands).reshape(1, 64, 1, 4096)


def solution(mesh):
    return jax.shard_map(
        per_device,
        mesh=mesh,
        in_specs=(P(None, "tr", None, "ct"), P(None, "ct", None, "tr"), P()),
        out_specs=P("ct", "tr", None, None),
        check_vma=False,
    )
```
